128 devices in a mesh: expert: 16 (over z, x), tensor: 8 (over y, core).
Axes of the slice: x: 4, y: 4, z: 4, core: 2. Of those that a mesh axis runs over, the one named last changes fastest.
Arguments:
- tokens: bfloat16 [2048, 4096], P('expert'), may hold values from -6 to 6
- cotangent: bfloat16 [2048, 4096], P('expert'), may hold values from -6 to 6
- expert_ids: int32 [2048, 8], P('expert'), may hold values from 0 to 127, all different within a row; in each aligned block of 128 rows (0 to 127, 128 to 255, ...) at most 9 rows name the same one
- gate_probs: float32 [2048, 8], P('expert'), may hold values from 0.05 to 1
- w_gate: bfloat16 [128, 896, 4096], P('expert', 'tensor'), may hold values from -0.09375 to 0.09375
- w_up: bfloat16 [128, 896, 4096], P('expert', 'tensor'), may hold values from -0.09375 to 0.09375
- w_down: bfloat16 [128, 896, 4096], P('expert', 'tensor'), may hold values from -0.1875 to 0.1875
Outputs:
- mixed: bfloat16 [2048, 4096], P('expert')
- grad_tokens: bfloat16 [2048, 4096], P('expert')
The draws below stay inside these ranges and needn't reach their ends.
Inputs may be any that keep to these rules, and one draw needn't show every extreme that they name: `expert_ids`: each token names 8 different experts; the 128 tokens of one index of the expert axis name one expert at most 9 times, a bound that some block reaches.
All inputs are finite; a program needn't handle non-finite values.
Results may differ from the reference program's by a relative error of at most 0.017.
Values may be sent and summed in bfloat16 or wider, within the bound.
A program may use at most 192 MiB of HBM per device.

```python
import math
import jax
import jax.numpy as jnp
import numpy as np
from jax import lax

D = 4096
HID = 896
TOP = 8
TOK_DEV = 128
EXPERTS = 128
TOKENS = 2048
CAP = 9
N_EXPERT = 16
N_TENSOR = 8


def level_of(stream_key, extent, cuts, smallest, largest):
    level, own = 1.0, jax.random.fold_in(stream_key, 6)
    for position, shards_of in cuts:
        heights = jnp.exp(jax.random.uniform(jax.random.fold_in(own, position), (shards_of,), jnp.float32, smallest / len(cuts), largest / len(cuts)))
        level = level * jnp.repeat(heights, extent[position] // shards_of).reshape([-1 if axis == position else 1 for axis in range(len(extent))])
    return level


def shared_out(key, own, number, rows, count, top, reach, slope):
    order = jax.random.permutation(key, count)
    crowded, usual = portions_of(count, rows * top, reach, slope, True), portions_of(count, rows * top, reach, slope, False)
    places = jnp.arange(count)

    def named(sizes, rotation):
        used = int((sizes > 0).sum())
        fixed = max(1, used // 4)
        shifted = fixed + (places - fixed + rotation * (used - fixed)) % max(1, count - fixed)
        return jnp.zeros((count,), jnp.int32).at[order[jnp.where(places < fixed, places, shifted)]].set(jnp.asarray(sizes, jnp.int32))

    sizes = jnp.where(number % 4 == 0, named(crowded, number // 4), named(usual, number - number // 4 - 1))
    mixed = jax.random.permutation(jax.random.fold_in(own, 3), count)
    donor, taker = mixed[0:count // 2 * 2:2], mixed[1:count // 2 * 2:2]
    slack = jnp.minimum(sizes[donor] - 1, reach - sizes[taker]) // 2
    slack = jnp.where((donor == order[0]) | (taker == order[0]) | (sizes[taker] == 0), 0, jnp.maximum(slack, 0))
    shifted = jax.random.randint(jax.random.fold_in(own, 4), (count // 2,), 0, 1 << 20) % (slack + 1)
    sizes = sizes.at[donor].add(-shifted).at[taker].add(shifted)
    items = jnp.searchsorted(jnp.cumsum(sizes), jnp.arange(rows * top), side="right").astype(jnp.int32)
    table = items.reshape(top, rows).T
    table = table[jax.random.permutation(jax.random.fold_in(own, 1), rows)]
    rotation = jax.random.randint(jax.random.fold_in(own, 2), (rows, 1), 0, top)
    return jnp.take_along_axis(table, (jnp.arange(top)[None, :] + rotation) % top, axis=1)


def portions_of(amount, total, most, slope, full):
    loads = [(1 << 20) // math.isqrt(rank ** slope) + 1 for rank in range(1, amount + 1)]
    largest = most if full else min(most, max(-(-total // amount), total * loads[0] // sum(loads)))
    least = 1 if total - largest >= amount - 1 else 0
    given, rest = [largest] + [least] * (amount - 1), total - largest - least * (amount - 1)
    while rest > 0:
        free = [i for i in range(1, amount) if given[i] < largest] or [i for i in range(1, amount) if given[i] < most]
        pool, remaining = sum([loads[i] for i in free]), rest
        for i in free:
            addition = min(most - given[i], max(1, remaining * loads[i] // pool), rest)
            given[i] = given[i] + addition
            rest = rest - addition
    return np.array(given)


def centred(key, extent, spread, reach, split=(), held_as=jnp.bfloat16):
    entries = spread * jax.random.normal(key, extent, jnp.float32)
    if split:
        entries = entries * level_of(key, extent, split, -0.22, 0.18)
    return jnp.clip(entries, -reach, reach).astype(held_as)


def setup_inputs(seed: int = 0) -> dict:
    key_list = jax.random.split(jax.random.key(seed), 8)
    tokens = centred(key_list[0], (TOKENS, D), 1.0, 6.0, ((0, 16),))
    cotangent = centred(key_list[1], (TOKENS, D), 1.0, 6.0, ((0, 16),))
    expert_ids_keys = jax.random.split(jax.random.fold_in(key_list[2], 1), TOKENS // TOK_DEV)
    expert_ids_turns = jax.random.permutation(jax.random.fold_in(key_list[2], 3), TOKENS // TOK_DEV)
    expert_ids = jax.vmap(lambda own, number: shared_out(jax.random.fold_in(key_list[2], 2), own, number, TOK_DEV, EXPERTS, TOP, CAP, 2))(expert_ids_keys, expert_ids_turns).reshape((TOKENS, TOP))
    gate_probs = jnp.clip(jnp.exp(math.log(1.0) - 2.9957323 * jax.random.uniform(key_list[3], (TOKENS, TOP), jnp.float32) ** level_of(key_list[3], (TOKENS, TOP), ((0, 16),), -0.2, 0.2)), 0.05, 1.0)
    w_gate = centred(key_list[4], (EXPERTS, HID, D), D ** -0.5, 0.09375, ((0, 16), (1, 8)))
    w_up = centred(key_list[5], (EXPERTS, HID, D), D ** -0.5, 0.09375, ((0, 16), (1, 8)))
    w_down = centred(key_list[6], (EXPERTS, HID, D), HID ** -0.5, 0.1875, ((0, 16), (1, 8)))
    return dict(tokens=tokens, cotangent=cotangent, expert_ids=expert_ids, gate_probs=gate_probs, w_gate=w_gate, w_up=w_up, w_down=w_down)


def block_product(operand, matrix, operand_two, matrix_two):
    row_count = operand.shape[0]
    block_size = matrix.shape[0] // N_TENSOR
    partial_value = jnp.einsum("rbh,bhd->rbd", operand.astype(jnp.float32).reshape(row_count, N_TENSOR, block_size), matrix.astype(jnp.float32).reshape(N_TENSOR, block_size, matrix.shape[1]))
    if operand_two is not None:
        partial_value = partial_value + jnp.einsum("rbh,bhd->rbd", operand_two.astype(jnp.float32).reshape(row_count, N_TENSOR, block_size), matrix_two.astype(jnp.float32).reshape(N_TENSOR, block_size, matrix_two.shape[1]))
    rounded = lax.optimization_barrier(partial_value.astype(jnp.bfloat16))
    return jnp.sum(rounded.astype(jnp.float32), axis=1).astype(jnp.bfloat16)


def reference(tokens, cotangent, expert_ids, gate_probs, w_gate, w_up, w_down):
    features = tokens.shape[1]
    pair_count = TOK_DEV * TOP
    flat_ids = expert_ids.reshape(N_EXPERT, pair_count)
    one_hot = (flat_ids[:, :, None] == jnp.arange(EXPERTS, dtype=jnp.int32)[None, None, :]).astype(jnp.int32)
    slot_index = jnp.sum(jnp.cumsum(one_hot, axis=1) * one_hot, axis=2) - 1
    source = jnp.arange(N_EXPERT, dtype=jnp.int32)[:, None] * jnp.ones((1, pair_count), jnp.int32)
    table_pos = (source * CAP + slot_index).astype(jnp.int32)
    token_index = (source * TOK_DEV + (jnp.arange(pair_count, dtype=jnp.int32) // TOP)[None, :]).astype(jnp.int32)
    row_table = jnp.full((EXPERTS, N_EXPERT * CAP), TOKENS, jnp.int32).at[flat_ids, table_pos].set(token_index)
    prob_table = jnp.zeros((EXPERTS, N_EXPERT * CAP), jnp.float32).at[flat_ids, table_pos].set(gate_probs.reshape(N_EXPERT, pair_count))
    tok_pad = jnp.concatenate([tokens, jnp.zeros((1, features), tokens.dtype)], 0)
    cot_pad = jnp.concatenate([cotangent, jnp.zeros((1, features), cotangent.dtype)], 0)

    def per_expert(packed):
        row_ids, prob_rows, gate_matrix, up_matrix, down_matrix = packed
        token_rows = tok_pad[row_ids]
        scaled_rows = (prob_rows[:, None] * cot_pad[row_ids].astype(jnp.float32)).astype(jnp.bfloat16)
        pre_gate = jnp.dot(token_rows, gate_matrix.T, preferred_element_type=jnp.float32)
        up_value = jnp.dot(token_rows, up_matrix.T, preferred_element_type=jnp.float32)
        sigmoid_gate = jax.nn.sigmoid(pre_gate)
        activated = pre_gate * sigmoid_gate
        hidden = (activated * up_value).astype(jnp.bfloat16)
        output_rows = block_product(hidden, down_matrix, None, None)
        grad_hidden = jnp.dot(scaled_rows, down_matrix.T, preferred_element_type=jnp.float32)
        grad_gate = (grad_hidden * up_value * sigmoid_gate * (1.0 + pre_gate * (1.0 - sigmoid_gate))).astype(jnp.bfloat16)
        grad_up = (grad_hidden * activated).astype(jnp.bfloat16)
        grad_rows = block_product(grad_gate, gate_matrix, grad_up, up_matrix)
        return output_rows, grad_rows

    outputs, gradients = lax.map(per_expert, (row_table, prob_table, w_gate, w_up, w_down))
    picked_out = outputs[flat_ids, table_pos].reshape(TOKENS, TOP, features)
    picked_grad = gradients[flat_ids, table_pos].reshape(TOKENS, TOP, features)
    mixed = jnp.einsum("nk,nkd->nd", gate_probs.astype(jnp.float32), picked_out.astype(jnp.float32)).astype(jnp.bfloat16)
    grad_tokens = jnp.sum(picked_grad.astype(jnp.float32), axis=1).astype(jnp.bfloat16)
    return mixed, grad_tokens
```

```python
import jax
import jax.numpy as jnp
from jax import lax
from jax.experimental import pallas as pl
from jax.experimental.pallas import tpu as pltpu
from jax.sharding import PartitionSpec as P

BF = jnp.bfloat16
F32 = jnp.float32
RING = 4
PEERS = 16
SLOTS = 8
MESH = pl.DeviceIdType.MESH


def flat_rows(block):
    groups, rows, width = block.shape
    return block.astype(F32).reshape(groups * rows, width).astype(BF)


def kernel(
    send, coll_hi, coll_lo, coll_one, perm, perm_back, wg, wu, wd,
    mixed_ref, grad_ref,
    x, wv, xs, xov, acc, accx, hid, rel, own_in, ret, comb, fin,
    a2a_s, a2a_r, ag_s, ag_r, rl_s, rl_r, wl, wx_s, wx_r,
    ac_s, ac_r, hd_s, hd_r, h_s, h_r, o_s, o_r, b_s, b_r, fy_s, fy_r, fs_s, fs_r,
):
    e, t = lax.axis_index("expert"), lax.axis_index("tensor")
    ez, ex = e // RING, e % RING
    y, c = t // 2, t % 2
    right_y, left_y, far_y = (y + 1) % RING, (y + 3) % RING, (y + 2) % RING
    right, left, sib = right_y * 2 + c, left_y * 2 + c, y * 2 + 1 - c
    half = xs.shape[1] // 2
    core_width = half * RING

    def to_of(k):
        return ((ez + k // RING) % RING) * RING + (ex + k % RING) % RING

    def from_of(k):
        return ((ez + RING - k // RING) % RING) * RING + (ex + RING - k % RING) % RING

    def remote(src, dst, ssem, rsem, pe, pt):
        return pltpu.make_async_remote_copy(
            src_ref=src, dst_ref=dst, send_sem=ssem, recv_sem=rsem,
            device_id={"expert": pe, "tensor": pt}, device_id_type=MESH,
        )

    mats = (wg, wu, wd)
    hu = wg.shape[1]

    def w_local(g, v):
        cols = pl.ds(pl.multiple_of(c * core_width + v * half, half), half)
        return pltpu.make_async_copy(
            mats[g].at[:, :, cols], wv.at[g, v, :, pl.ds(0, hu), :], wl.at[g, v]
        )

    def w_cross(g, v):
        cols = pl.ds(pl.multiple_of((1 - c) * core_width + v * half, half), half)
        return remote(
            mats[g].at[:, :, cols], wv.at[g, v, :, pl.ds(128, hu), :],
            wx_s.at[g, v], wx_r.at[g, v], e, sib,
        )

    for g in range(3):
        for v in range(RING):
            w_local(g, v).start()

    barrier = pltpu.get_barrier_semaphore()

    @pl.loop(1, PEERS)
    def _(k):
        pl.semaphore_signal(
            barrier, inc=1, device_id={"expert": to_of(k), "tensor": t}, device_id_type=MESH
        )

    for other in (right, left, sib):
        pl.semaphore_signal(
            barrier, inc=1, device_id={"expert": e, "tensor": other}, device_id_type=MESH
        )
    pl.semaphore_wait(barrier, PEERS + 2)

    def a2a(k):
        dst = to_of(k)
        return remote(send.at[dst], x.at[y, :, e], a2a_s.at[k], a2a_r.at[k], dst, t)

    def a2a_in(k):
        return remote(send.at[e], x.at[y, :, from_of(k)], a2a_s.at[k], a2a_r.at[k], to_of(k), t)

    first = pltpu.make_async_copy(send.at[e], x.at[y, :, e], a2a_r.at[0])
    first.start()

    @pl.loop(1, PEERS)
    def _(k):
        a2a(k).start()

    for v in range(RING):
        for g in range(3):
            w_cross(g, v).start()

    zeros = jnp.zeros((8, 16, half), BF)
    for g in range(3):
        for v in range(RING):
            wv[g, v, :, hu:128, :] = zeros
            wv[g, v, :, 128 + hu:256, :] = zeros

    def go_right(k):
        s = from_of(k)
        return remote(x.at[y, :, s], x.at[y, :, s], ag_s.at[0, k], ag_r.at[0, k], e, right)

    def go_left(k):
        s = from_of(k)
        return remote(x.at[y, :, s], x.at[y, :, s], ag_s.at[1, k], ag_r.at[1, k], e, left)

    def from_left(k):
        s = from_of(k)
        return remote(x.at[y, :, s], x.at[left_y, :, s], ag_s.at[0, k], ag_r.at[0, k], e, right)

    def from_right(k):
        s = from_of(k)
        return remote(x.at[y, :, s], x.at[right_y, :, s], ag_s.at[1, k], ag_r.at[1, k], e, left)

    def relay_right(k):
        s = from_of(k)
        return remote(x.at[left_y, :, s], x.at[left_y, :, s], rl_s.at[k], rl_r.at[k], e, right)

    def relay_left(k):
        s = from_of(k)
        return remote(x.at[right_y, :, s], x.at[right_y, :, s], rl_s.at[k], rl_r.at[k], e, left)

    def relay_in(k):
        s = from_of(k)
        return remote(x.at[left_y, :, s], x.at[far_y, :, s], rl_s.at[k], rl_r.at[k], e, right)

    first.wait()
    go_right(0).start()
    go_left(0).start()

    @pl.loop(1, PEERS)
    def _(k):
        a2a_in(k).wait_recv()
        go_right(k).start()
        go_left(k).start()

    for v in range(RING):
        for g in range(3):
            w_local(g, v).wait()
            w_cross(g, v).wait_recv()

    def acc_swap(i):
        return remote(
            acc.at[:, i, :, pl.ds(128, 128)], accx.at[:, i], ac_s.at[i], ac_r.at[i], e, sib
        )

    def contract(v, start, end):
        xov[...] = jnp.dot(perm[...], flat_rows(x[v, 8]), preferred_element_type=F32).astype(BF)

        @pl.loop(0, 8)
        def _(i):
            xs[0:128, :] = flat_rows(x[v, i])
            xs[128:144, :] = xov[pl.ds(pl.multiple_of(i * 16, 16), 16), :]
            for g in range(3):
                rows = xs[:, 0:half] if g < 2 else xs[:, half:]
                part = lax.dot_general(
                    rows, wv[g, v, i], (((1,), (1,)), ((), ())), preferred_element_type=F32
                )
                if start:
                    acc[g, i] = part
                else:
                    acc[g, i] = acc[g, i] + part
            if end:
                acc_swap(i).start()

    contract(y, True, False)

    @pl.loop(0, PEERS // 2)
    def _(j):
        even, odd = 2 * j, 2 * j + 1
        from_left(even).wait_recv()
        relay_right(even).start()
        from_right(even).wait_recv()
        from_right(odd).wait_recv()
        relay_left(odd).start()
        from_left(odd).wait_recv()

    contract(left_y, False, False)
    contract(right_y, False, False)

    @pl.loop(0, PEERS)
    def _(k):
        relay_in(k).wait_recv()

    contract(far_y, False, True)

    @pl.loop(0, PEERS)
    def _(k):
        go_right(k).wait_send()
        go_left(k).wait_send()
        relay_right(k).wait_send()

    def hid_swap(i):
        return remote(
            hid.at[:, i, :, pl.ds(0, 128)], hid.at[:, i, :, pl.ds(128, 128)],
            hd_s.at[i], hd_r.at[i], e, sib,
        )

    @pl.loop(0, 8)
    def _(i):
        acc_swap(i).wait_recv()
        pre = acc[0, i, :, 0:128] + accx[0, i]
        up = acc[1, i, :, 0:128] + accx[1, i]
        gh = acc[2, i, :, 0:128] + accx[2, i]
        sg = jax.nn.sigmoid(pre)
        act = pre * sg
        hid[0, i, :, 0:128] = (act * up).astype(BF)
        hid[1, i, :, 0:128] = (gh * up * sg * (1.0 + pre * (1.0 - sg))).astype(BF)
        hid[2, i, :, 0:128] = (gh * act).astype(BF)
        hid_swap(i).start()

    @pl.loop(0, 8)
    def _(i):
        hid_swap(i).wait_recv()

    def expand(v):
        @pl.loop(0, 8)
        def _(i):
            out = jnp.dot(hid[0, i], wv[2, v, i], preferred_element_type=F32)
            x[v, i, :, :, 0:half] = out[0:128].reshape(PEERS, SLOTS, half).astype(BF)
            tail = pl.ds(pl.multiple_of(i * 16, 16), 16)
            xov[tail, 0:half] = out[128:144].astype(BF)
            grad = jnp.dot(hid[1, i], wv[0, v, i], preferred_element_type=F32)
            grad = grad + jnp.dot(hid[2, i], wv[1, v, i], preferred_element_type=F32)
            x[v, i, :, :, half:] = grad[0:128].reshape(PEERS, SLOTS, half).astype(BF)
            xov[tail, half:] = grad[128:144].astype(BF)

        over = jnp.dot(perm_back[...], xov[...], preferred_element_type=F32)
        x[v, 8] = over.reshape(PEERS, SLOTS, 2 * half).astype(BF)

    def far_right(k):
        return remote(x.at[far_y, :, from_of(k)], rel.at[k], h_s.at[k], h_r.at[k], e, right)

    def far_left(k):
        return remote(x.at[far_y, :, from_of(k)], rel.at[k], h_s.at[k], h_r.at[k], e, left)

    def near_right(k):
        return remote(
            x.at[right_y, :, from_of(k)], own_in.at[0, k], o_s.at[0, k], o_r.at[0, k], e, right
        )

    def near_left(k):
        return remote(
            x.at[left_y, :, from_of(k)], own_in.at[1, k], o_s.at[1, k], o_r.at[1, k], e, left
        )

    expand(far_y)

    @pl.loop(0, PEERS // 2)
    def _(j):
        far_right(2 * j).start()
        far_left(2 * j + 1).start()

    expand(right_y)

    @pl.loop(0, PEERS // 2)
    def _(j):
        near_right(2 * j + 1).start()

    expand(left_y)

    @pl.loop(0, PEERS // 2)
    def _(j):
        near_left(2 * j).start()

    expand(y)

    @pl.loop(0, PEERS // 2)
    def _(j):
        even, odd = 2 * j, 2 * j + 1
        far_right(even).wait_recv()
        s = from_of(even)
        x[right_y, :, s] = (x[right_y, :, s].astype(F32) + rel[even].astype(F32)).astype(BF)
        near_right(even).start()
        far_left(odd).wait_recv()
        s = from_of(odd)
        x[left_y, :, s] = (x[left_y, :, s].astype(F32) + rel[odd].astype(F32)).astype(BF)
        near_left(odd).start()

    def back(k):
        s = from_of(k)
        return remote(x.at[y, :, s], ret.at[e], b_s.at[k], b_r.at[k], s, t)

    def back_in(k):
        return remote(x.at[y, :, e], ret.at[to_of(k)], b_s.at[k], b_r.at[k], from_of(k), t)

    def own_sum(k):
        near_right(k).wait_recv()
        near_left(k).wait_recv()
        total = x[y, :, from_of(k)].astype(F32) + own_in[0, k].astype(F32)
        return (total + own_in[1, k].astype(F32)).astype(BF)

    ret[e] = own_sum(0)

    @pl.loop(1, PEERS)
    def _(k):
        x[y, :, from_of(k)] = own_sum(k)
        back(k).start()

    def combine(d):
        rows = flat_rows(ret[d])
        low = rows[:, 0:half]
        part = jnp.dot(coll_hi[d], low, preferred_element_type=F32)
        part = part + jnp.dot(coll_lo[d], low, preferred_element_type=F32)
        return part, jnp.dot(coll_one[d], rows[:, half:], preferred_element_type=F32)

    comb[:, 0:half], comb[:, half:] = combine(e)

    @pl.loop(1, PEERS)
    def _(k):
        back_in(k).wait_recv()
        m, g = combine(to_of(k))
        comb[:, 0:half] = comb[:, 0:half] + m
        comb[:, half:] = comb[:, half:] + g

    fin[t] = comb[...].astype(BF)

    rows_a, rows_b = pl.ds(0, 64), pl.ds(64, 64)
    left_t, right_t, far_t = left, right, far_y * 2 + c

    def fin_y(n, slot, rows, peer):
        ref = fin.at[slot, rows, :]
        return remote(ref, ref, fy_s.at[n], fy_r.at[n], e, peer)

    def fin_s(n, slot, rows):
        ref = fin.at[slot, rows, :]
        return remote(ref, ref, fs_s.at[n], fs_r.at[n], e, sib)

    full = pl.ds(0, 128)
    out_right, out_left = fin_y(0, t, full, right), fin_y(1, t, full, left)
    out_right.start()
    out_left.start()
    sends = [fin_s(0, t, full)]
    sends[0].start()
    fin_y(0, left_t, full, right).wait_recv()
    hop_right = fin_y(2, left_t, rows_a, right)
    hop_right.start()
    sends.append(fin_s(1, left_t, full))
    sends[1].start()
    fin_y(1, right_t, full, left).wait_recv()
    hop_left = fin_y(3, right_t, rows_b, left)
    hop_left.start()
    sends.append(fin_s(2, right_t, full))
    sends[2].start()
    fin_y(2, far_t, rows_a, right).wait_recv()
    sends.append(fin_s(3, far_t, rows_a))
    sends[3].start()
    fin_y(3, far_t, rows_b, left).wait_recv()
    sends.append(fin_s(4, far_t, rows_b))
    sends[4].start()
    for copy in sends:
        copy.wait()
    for copy in (out_right, out_left, hop_right, hop_left):
        copy.wait_send()

    @pl.loop(1, PEERS)
    def _(k):
        a2a(k).wait_send()
        back(k).wait_send()

    @pl.loop(0, PEERS)
    def _(k):
        far_right(k).wait_send()
        near_right(k).wait_send()
        near_left(k).wait_send()

    @pl.loop(0, 8)
    def _(i):
        acc_swap(i).wait_send()
        hid_swap(i).wait_send()

    for g in range(3):
        for v in range(RING):
            w_cross(g, v).wait_send()

    for slot in range(2 * RING):
        off = (slot % 2) * core_width + (slot // 2) * half
        mixed_ref[:, off:off + half] = fin[slot, :, 0:half]
        grad_ref[:, off:off + half] = fin[slot, :, half:]


def expert_kernel(send, coll_hi, coll_lo, coll_one, perm, perm_back, w_gate, w_up, w_down):
    width = send.shape[-1]
    half = width // 2
    tok = coll_hi.shape[1]
    features = w_gate.shape[2]
    dma = pltpu.SemaphoreType.DMA
    vmem = pl.BlockSpec(memory_space=pltpu.VMEM)
    hbm = pl.BlockSpec(memory_space=pltpu.HBM)
    return pl.pallas_call(
        kernel,
        out_shape=[jax.ShapeDtypeStruct((tok, features), BF)] * 2,
        in_specs=[vmem] * 6 + [hbm] * 3,
        out_specs=[vmem] * 2,
        scratch_shapes=[
            pltpu.VMEM((RING, 9, PEERS, SLOTS, width), BF),
            pltpu.VMEM((3, RING, 8, 256, half), BF),
            pltpu.VMEM((144, width), BF),
            pltpu.VMEM((128, width), BF),
            pltpu.VMEM((3, 8, 144, 256), F32),
            pltpu.VMEM((3, 8, 144, 128), F32),
            pltpu.VMEM((3, 8, 144, 256), BF),
            pltpu.VMEM((PEERS, 9, SLOTS, width), BF),
            pltpu.VMEM((2, PEERS, 9, SLOTS, width), BF),
            pltpu.VMEM((PEERS, 9, SLOTS, width), BF),
            pltpu.VMEM((tok, width), F32),
            pltpu.VMEM((2 * RING, tok, width), BF),
            dma((PEERS,)), dma((PEERS,)),
            dma((2, PEERS)), dma((2, PEERS)),
            dma((PEERS,)), dma((PEERS,)),
            dma((3, RING)), dma((3, RING)), dma((3, RING)),
            dma((8,)), dma((8,)), dma((8,)), dma((8,)),
            dma((PEERS,)), dma((PEERS,)),
            dma((2, PEERS)), dma((2, PEERS)),
            dma((PEERS,)), dma((PEERS,)),
            dma((4,)), dma((4,)), dma((5,)), dma((5,)),
        ],
        compiler_params=pltpu.CompilerParams(
            collective_id=0, has_side_effects=True, vmem_limit_bytes=66 * 1000 * 1000
        ),
    )(send, coll_hi, coll_lo, coll_one, perm, perm_back, w_gate, w_up, w_down)


def by_group(table, devs):
    experts, cap, tok = table.shape
    table = table.reshape(devs, experts // devs, cap, tok)
    main = table[:, :, :8].reshape(devs, (experts // devs) * 8, tok)
    return jnp.concatenate([main, table[:, :, 8]], axis=1)


def body(tokens, cotangent, expert_ids, gate_probs, w_gate, w_up, w_down):
    tok_count, features = tokens.shape
    devs = lax.axis_size("expert")
    local_experts = w_gate.shape[0]
    all_experts = local_experts * devs
    cap = 9
    slices = 2 * RING
    half = features // slices
    t = lax.axis_index("tensor")
    offset = (t % 2) * (features // 2) + (t // 2) * half
    matches = expert_ids[:, :, None] == jnp.arange(all_experts, dtype=jnp.int32)[None, None, :]
    chosen = jnp.any(matches, axis=1)
    prob_table = jnp.sum(jnp.where(matches, gate_probs[:, :, None], 0.0), axis=1)
    positions = jnp.arange(tok_count, dtype=jnp.int32)
    earlier = (positions[:, None] > positions[None, :]).astype(BF)
    slot_table = jnp.dot(earlier, chosen.astype(BF), preferred_element_type=F32)
    slot_ids = jnp.arange(cap, dtype=F32)
    place = chosen.T[:, None, :] & (slot_table.T[:, None, :] == slot_ids[None, :, None])
    place = by_group(place, devs)
    prob_rows = by_group(
        jnp.broadcast_to(prob_table.T[:, None, :], (all_experts, cap, tok_count)), devs
    )
    weights = jnp.where(place, prob_rows, 0.0)
    row_prob = jnp.sum(weights, axis=-1, keepdims=True)
    one = place.astype(BF)
    tok_part = lax.dynamic_slice_in_dim(tokens, offset, half, 1)
    cot_part = lax.dynamic_slice_in_dim(cotangent, offset, half, 1)
    token_rows = jnp.einsum("dst,tf->dsf", one, tok_part, preferred_element_type=F32).astype(BF)
    cot_rows = jnp.einsum("dst,tf->dsf", one, cot_part, preferred_element_type=F32)
    scaled_rows = (cot_rows * row_prob).astype(BF)
    send = jnp.concatenate([token_rows, scaled_rows], axis=-1)
    send = send.reshape(devs, cap, SLOTS, 2 * half)
    weights = weights.transpose(0, 2, 1)
    rounded = lax.reduce_precision(weights, 8, 7)
    coll_hi = rounded.astype(BF)
    coll_lo = (weights - rounded).astype(BF)
    coll_one = one.transpose(0, 2, 1)
    order = jnp.arange(devs * local_experts, dtype=jnp.int32)
    source = (order % devs) * local_experts + order // devs
    perm = (source[:, None] == order[None, :]).astype(BF)
    return tuple(
        expert_kernel(send, coll_hi, coll_lo, coll_one, perm, perm.T, w_gate, w_up, w_down)
    )


def solution(mesh):
    return jax.shard_map(
        body,
        mesh=mesh,
        in_specs=(
            P("expert", None),
            P("expert", None),
            P("expert", None),
            P("expert", None),
            P("expert", "tensor", None),
            P("expert", "tensor", None),
            P("expert", "tensor", None),
        ),
        out_specs=(P("expert", None), P("expert", None)),
        check_vma=False,
    )
```

```python
import jax
import jax.numpy as jnp
from jax import lax
from jax.experimental import pallas as pl
from jax.experimental.pallas import tpu as pltpu
from jax.sharding import PartitionSpec as P

BF = jnp.bfloat16
F32 = jnp.float32
RING = 4
PEERS = 16
SLOTS = 8
AXIAL = 6
DIAG = 9
ROWS = 72
MESH = pl.DeviceIdType.MESH


def flat_rows(block):
    return block.astype(F32).reshape(-1, block.shape[-1]).astype(BF)


def kernel(
    tokens, cotangent, ids_ref, probs_ref, perm, perm_back, wg, wu, wd,
    mixed_ref, grad_ref,
    tok, cot, slot_ref, prob_ref, one_d, wrow_d, wrow_g, coll_d, coll_g,
    sendg, sendd, x, wv, xs, xov, acc, accx, hid, rel, own_in, ret, retd, comb, combs, combr, fin,
    tk, g_s, g_r, d_s, d_r, ag_s, ag_r, rl_s, rl_r, wl, wx_s, wx_r,
    ac_s, ac_r, hd_s, hd_r, h_s, h_r, o_s, o_r, b_s, b_r, rd_s, rd_r, cs_s, cs_r,
    fy_s, fy_r, fs_s, fs_r, out_sem,
):
    e, t = lax.axis_index("expert"), lax.axis_index("tensor")
    ez, ex = e // RING, e % RING
    y, c = t // 2, t % 2
    right_y, left_y, far_y = (y + 1) % RING, (y + 3) % RING, (y + 2) % RING
    right, left, sib, far = right_y * 2 + c, left_y * 2 + c, y * 2 + 1 - c, far_y * 2 + c
    half = xs.shape[1] // 2
    core_width = half * RING

    def to_of(k):
        return ((ez + k // RING) % RING) * RING + (ex + k % RING) % RING

    def from_of(k):
        return ((ez + RING - k // RING) % RING) * RING + (ex + RING - k % RING) % RING

    def axial(j):
        return (j % 3 + 1) * (1 + 3 * (j // 3))

    def diag(j):
        return (1 + j // 3) * RING + 1 + j % 3

    def remote(src, dst, ssem, rsem, pe, pt):
        return pltpu.make_async_remote_copy(
            src_ref=src, dst_ref=dst, send_sem=ssem, recv_sem=rsem,
            device_id={"expert": pe, "tensor": pt}, device_id_type=MESH,
        )

    def signal(pe, pt):
        pl.semaphore_signal(
            pltpu.get_barrier_semaphore(), inc=1,
            device_id={"expert": pe, "tensor": pt}, device_id_type=MESH,
        )

    mats = (wg, wu, wd)
    hu = wg.shape[1]

    def columns(core, v):
        return pl.ds(pl.multiple_of(core * core_width + v * half, half), half)

    def w_local(g, v):
        return pltpu.make_async_copy(
            mats[g].at[:, :, columns(c, v)], wv.at[g, v, :, pl.ds(0, hu), :], wl.at[g, v]
        )

    def w_cross(g, v):
        return remote(
            mats[g].at[:, :, columns(1 - c, v)], wv.at[g, v, :, pl.ds(128, hu), :],
            wx_s.at[g, v], wx_r.at[g, v], e, sib,
        )

    def t_local(n, v):
        src, dst = ((tokens, tok), (cotangent, cot))[n]
        return pltpu.make_async_copy(src.at[:, columns(c, v)], dst.at[v], tk.at[n, v])

    for v in range(RING):
        for n in range(2):
            t_local(n, v).start()

    @pl.loop(1, PEERS)
    def _(k):
        signal(to_of(k), t)

    for other in (right, left, far, sib):
        signal(e, other)

    for g in range(3):
        for v in range(RING):
            w_local(g, v).start()

    count = ids_ref.shape[0]
    lane = lax.broadcasted_iota(jnp.int32, (count, count), 1)
    line = lax.broadcasted_iota(jnp.int32, (count, count), 0)
    chosen = jnp.zeros((count, count), F32)
    prob = jnp.zeros((count, count), F32)
    for k in range(ids_ref.shape[1]):
        match = ids_ref[:, k:k + 1] == lane
        chosen = chosen + match.astype(F32)
        prob = prob + jnp.where(match, probs_ref[:, k:k + 1], 0.0)
    chosen = chosen.T
    before = (line < lane).astype(F32).astype(BF)
    slot = jnp.dot(chosen.astype(BF), before, preferred_element_type=F32)
    slot_ref[...] = jnp.where(chosen > 0.5, slot, -1.0)
    prob_ref[...] = prob.T

    def row_block(j):
        return pl.ds(pl.multiple_of(j * ROWS, SLOTS), ROWS)

    def build(d):
        block = pl.ds(pl.multiple_of(d * SLOTS, SLOTS), SLOTS)
        slots, weights = slot_ref[block, :], prob_ref[block, :]
        number = lax.broadcasted_iota(jnp.int32, (SLOTS, count), 0).astype(F32)
        place, weight = [], []
        for i in range(SLOTS):
            hit = slots[i:i + 1, :] == number
            place.append(hit.astype(F32))
            weight.append(jnp.where(hit, weights[i:i + 1, :], 0.0))
        hit = slots == float(SLOTS)
        place.append(hit.astype(F32))
        weight.append(jnp.where(hit, weights, 0.0))
        return jnp.concatenate(place, axis=0), jnp.concatenate(weight, axis=0)

    def fill(ref, one, weight, v):
        total = jnp.sum(weight, axis=1, keepdims=True)
        rows = jnp.dot(one, tok[v], preferred_element_type=F32)
        ref[:, :, 0:half] = rows.reshape(9, SLOTS, half).astype(BF)
        rows = jnp.dot(one, cot[v], preferred_element_type=F32) * total
        ref[:, :, half:] = rows.reshape(9, SLOTS, half).astype(BF)

    for n in range(2):
        for v in range(RING):
            t_local(n, v).wait()

    @pl.loop(0, DIAG)
    def _(j):
        place, weight = build(to_of(diag(j)))
        wrow_g[j // 3, row_block(j % 3), :] = weight
        fill(sendg.at[j], place.astype(BF), weight, y)

    pl.semaphore_wait(pltpu.get_barrier_semaphore(), PEERS + 3)

    def slice_out(j):
        return remote(sendg.at[j], x.at[y, :, e], g_s.at[j], g_r.at[j], to_of(diag(j)), t)

    def slice_in(j):
        s = from_of(diag(j))
        return remote(sendg.at[j], x.at[y, :, s], g_s.at[j], g_r.at[j], to_of(diag(j)), t)

    def whole_out(j, v):
        return remote(
            sendd.at[v, j], x.at[v, :, e], d_s.at[v, j], d_r.at[v, j], to_of(axial(j)), t
        )

    def whole_in(j, v):
        s = from_of(axial(j))
        return remote(
            sendd.at[v, j], x.at[v, :, s], d_s.at[v, j], d_r.at[v, j], to_of(axial(j)), t
        )

    @pl.loop(0, DIAG)
    def _(j):
        slice_out(j).start()

    @pl.loop(0, AXIAL)
    def _(j):
        place, weight = build(to_of(axial(j)))
        wrow_d[row_block(j), :] = weight
        one_d[j] = place.astype(BF)
        fill(sendd.at[y, j], one_d[j], weight, y)
        whole_out(j, y).start()

    for v in range(RING):
        for g in range(3):
            w_cross(g, v).start()

    def pushed(n, j, dst_y, peer):
        s = from_of(diag(j))
        return remote(x.at[y, :, s], x.at[dst_y, :, s], ag_s.at[n, j], ag_r.at[n, j], e, peer)

    def go_right(j):
        return pushed(0, j, y, right)

    def go_left(j):
        return pushed(1, j, y, left)

    def from_left(j):
        return pushed(0, j, left_y, right)

    def from_right(j):
        return pushed(1, j, right_y, left)

    def relay(j, slice_y, peer):
        s = from_of(diag(j))
        ref = x.at[slice_y, :, s]
        return remote(ref, ref, rl_s.at[j], rl_r.at[j], e, peer)

    @pl.loop(0, DIAG)
    def _(j):
        slice_in(j).wait_recv()
        go_right(j).start()
        go_left(j).start()
        for u in range(2):
            n = 2 * j + u
            q, jj = 1 + n // AXIAL, n % AXIAL
            v = (y + 2 * q - 1 - 3 * (q // 3)) % RING
            fill(sendd.at[v, jj], one_d[jj], wrow_d[row_block(jj), :], v)
            whole_out(jj, v).start()

    place, weight = build(e)
    wrow_d[row_block(AXIAL), :] = weight
    place = place.astype(BF)
    for v in range(RING):
        fill(x.at[v, :, e], place, weight, v)

    zeros = jnp.zeros((8, 16, half), BF)
    for g in range(3):
        for v in range(RING):
            wv[g, v, :, hu:128, :] = zeros
            wv[g, v, :, 128 + hu:256, :] = zeros

    for v in range(RING):
        for g in range(3):
            w_local(g, v).wait()
            w_cross(g, v).wait_recv()

    def acc_swap(i):
        return remote(
            acc.at[:, i, :, pl.ds(128, 128)], accx.at[:, i], ac_s.at[i], ac_r.at[i], e, sib
        )

    def contract(v, start, end):
        @pl.loop(0, AXIAL)
        def _(j):
            whole_in(j, v).wait_recv()

        xov[...] = jnp.dot(perm[...], flat_rows(x[v, 8]), preferred_element_type=F32).astype(BF)

        @pl.loop(0, 8)
        def _(i):
            xs[0:128, :] = flat_rows(x[v, i])
            xs[128:144, :] = xov[pl.ds(pl.multiple_of(i * 16, 16), 16), :]
            for g in range(3):
                rows = xs[:, 0:half] if g < 2 else xs[:, half:]
                part = lax.dot_general(
                    rows, wv[g, v, i], (((1,), (1,)), ((), ())), preferred_element_type=F32
                )
                if start:
                    acc[g, i] = part
                else:
                    acc[g, i] = acc[g, i] + part
            if end:
                acc_swap(i).start()

    def relay_even(j):
        from_left(j).wait_recv()
        relay(j, left_y, right).start()
        from_right(j).wait_recv()

    def relay_odd(j):
        from_right(j).wait_recv()
        relay(j, right_y, left).start()
        from_left(j).wait_recv()

    contract(y, True, False)

    @pl.loop(0, DIAG // 2)
    def _(j):
        relay_even(2 * j)
        relay_odd(2 * j + 1)

    relay_even(DIAG - 1)
    contract(right_y, False, False)
    contract(left_y, False, False)

    @pl.loop(0, DIAG)
    def _(j):
        relay(j, far_y, right).wait_recv()

    contract(far_y, False, True)

    @pl.loop(0, DIAG)
    def _(j):
        go_right(j).wait_send()
        go_left(j).wait_send()
        relay(j, left_y, right).wait_send()

    def hid_swap(i):
        return remote(
            hid.at[:, i, :, pl.ds(0, 128)], hid.at[:, i, :, pl.ds(128, 128)],
            hd_s.at[i], hd_r.at[i], e, sib,
        )

    @pl.loop(0, 8)
    def _(i):
        acc_swap(i).wait()
        pre = acc[0, i, :, 0:128] + accx[0, i]
        up = acc[1, i, :, 0:128] + accx[1, i]
        gh = acc[2, i, :, 0:128] + accx[2, i]
        sg = jax.nn.sigmoid(pre)
        act = pre * sg
        hid[0, i, :, 0:128] = (act * up).astype(BF)
        hid[1, i, :, 0:128] = (gh * up * sg * (1.0 + pre * (1.0 - sg))).astype(BF)
        hid[2, i, :, 0:128] = (gh * act).astype(BF)
        hid_swap(i).start()

    @pl.loop(0, 8)
    def _(i):
        hid_swap(i).wait_recv()

    def whole_back(j, v):
        s = from_of(axial(j))
        return remote(x.at[v, :, s], retd.at[v, j], rd_s.at[v, j], rd_r.at[v, j], s, t)

    def expand(v):
        @pl.loop(0, 8)
        def _(i):
            out = jnp.dot(hid[0, i], wv[2, v, i], preferred_element_type=F32)
            x[v, i, :, :, 0:half] = out[0:128].reshape(PEERS, SLOTS, half).astype(BF)
            tail = pl.ds(pl.multiple_of(i * 16, 16), 16)
            xov[tail, 0:half] = out[128:144].astype(BF)
            grad = jnp.dot(hid[1, i], wv[0, v, i], preferred_element_type=F32)
            grad = grad + jnp.dot(hid[2, i], wv[1, v, i], preferred_element_type=F32)
            x[v, i, :, :, half:] = grad[0:128].reshape(PEERS, SLOTS, half).astype(BF)
            xov[tail, half:] = grad[128:144].astype(BF)

        over = jnp.dot(perm_back[...], xov[...], preferred_element_type=F32)
        x[v, 8] = over.reshape(PEERS, SLOTS, 2 * half).astype(BF)

    def return_whole(v):
        @pl.loop(0, AXIAL)
        def _(j):
            whole_back(j, v).start()

    def far_out(j, peer):
        s = from_of(diag(j))
        return remote(x.at[far_y, :, s], rel.at[j], h_s.at[j], h_r.at[j], e, peer)

    def near(n, j, slice_y, peer):
        s = from_of(diag(j))
        return remote(x.at[slice_y, :, s], own_in.at[n, j], o_s.at[n, j], o_r.at[n, j], e, peer)

    def near_right(j):
        return near(0, j, right_y, right)

    def near_left(j):
        return near(1, j, left_y, left)

    def add_relayed(j, slice_y):
        far_out(j, right).wait_recv()
        s = from_of(diag(j))
        x[slice_y, :, s] = (x[slice_y, :, s].astype(F32) + rel[j].astype(F32)).astype(BF)

    expand(far_y)

    @pl.loop(0, DIAG // 2)
    def _(j):
        far_out(2 * j, right).start()
        far_out(2 * j + 1, left).start()

    far_out(DIAG - 1, right).start()
    return_whole(far_y)
    expand(right_y)
    near_right(1).start()
    return_whole(right_y)
    expand(left_y)
    near_left(0).start()
    return_whole(left_y)
    expand(y)
    return_whole(y)

    @pl.loop(0, DIAG // 2)
    def _(j):
        even, odd = 2 * j, 2 * j + 1
        add_relayed(even, right_y)
        near_right(even).start()
        near_left(even + 2).start()
        add_relayed(odd, left_y)
        near_left(odd).start()

        @pl.when(j < DIAG // 2 - 1)
        def _():
            near_right(odd + 2).start()

    add_relayed(DIAG - 1, right_y)
    near_right(DIAG - 1).start()

    def split(ref, weights):
        weights = weights.T
        hi = weights.astype(BF)
        ref[0] = hi
        ref[1] = (weights - hi.astype(F32)).astype(BF)
        ref[2] = (weights > 0.0).astype(F32).astype(BF)

    def gathered(coll, rows):
        width = rows.shape[0]
        low = rows[:, 0:half]
        part = jnp.dot(coll[0, :, 0:width], low, preferred_element_type=F32)
        part = part + jnp.dot(coll[1, :, 0:width], low, preferred_element_type=F32)
        return part, jnp.dot(coll[2, :, 0:width], rows[:, half:], preferred_element_type=F32)

    wrow_d[(AXIAL + 1) * ROWS:, :] = jnp.zeros((wrow_d.shape[0] - (AXIAL + 1) * ROWS, count), F32)
    split(coll_d, wrow_d[...])
    for n in range(3):
        wrow_g[n, 3 * ROWS:, :] = jnp.zeros((wrow_g.shape[1] - 3 * ROWS, count), F32)
        split(coll_g.at[n], wrow_g[n])

    def part_sum(n, slice_y):
        return remote(combs.at[n], combr.at[n], cs_s.at[n], cs_r.at[n], e, slice_y * 2 + c)

    for n, v in enumerate((far_y, right_y, left_y, y)):
        retd[v, AXIAL] = x[v, :, e]

        @pl.loop(0, AXIAL)
        def _(j, v=v):
            whole_back(j, v).wait_recv()

        m, g = gathered(coll_d, flat_rows(retd[v]))
        if n < 3:
            combs[n, :, 0:half] = m.astype(BF)
            combs[n, :, half:] = g.astype(BF)
            part_sum(n, v).start()
        else:
            comb[:, 0:half] = m
            comb[:, half:] = g

    def slice_back(j):
        s = from_of(diag(j))
        return remote(x.at[y, :, s], ret.at[j], b_s.at[j], b_r.at[j], s, t)

    @pl.loop(0, DIAG)
    def _(j):
        near_right(j).wait_recv()
        near_left(j).wait_recv()
        s = from_of(diag(j))
        total = x[y, :, s].astype(F32) + own_in[0, j].astype(F32)
        x[y, :, s] = (total + own_in[1, j].astype(F32)).astype(BF)
        slice_back(j).start()

    for n, v in enumerate((far_y, right_y, left_y)):
        part_sum(n, v).wait_recv()
        comb[...] = comb[...] + combr[n].astype(F32)
    for n in range(3):
        for j in range(3 * n, 3 * n + 3):
            slice_back(j).wait_recv()
        m, g = gathered(coll_g.at[n], flat_rows(ret[3 * n:3 * n + 3]))
        comb[:, 0:half] = comb[:, 0:half] + m
        comb[:, half:] = comb[:, half:] + g
    fin[t] = comb[...].astype(BF)

    rows_of = (pl.ds(0, 64), pl.ds(64, 64))

    def fin_copy(sems, n, slot_t, h, peer):
        ref = fin.at[slot_t, rows_of[h], :]
        return remote(ref, ref, sems[0].at[n], sems[1].at[n], e, peer)

    yy, ss = (fy_s, fy_r), (fs_s, fs_r)
    sends = []

    def push(sems, n, slot_t, h, peer):
        copy = fin_copy(sems, n, slot_t, h, peer)
        copy.start()
        sends.append(copy)

    push(yy, 0, t, 0, right)
    push(yy, 1, t, 1, left)
    push(yy, 2, t, 1, right)
    push(yy, 3, t, 0, left)
    push(ss, 0, t, 0, sib)
    push(ss, 1, t, 1, sib)
    fin_copy(yy, 0, left, 0, right).wait_recv()
    push(yy, 4, left, 0, right)
    push(ss, 2, left, 0, sib)
    fin_copy(yy, 1, right, 1, left).wait_recv()
    push(yy, 5, right, 1, left)
    push(ss, 3, right, 1, sib)
    fin_copy(yy, 2, left, 1, right).wait_recv()
    push(ss, 4, left, 1, sib)
    fin_copy(yy, 3, right, 0, left).wait_recv()
    push(ss, 5, right, 0, sib)
    fin_copy(yy, 4, far, 0, right).wait_recv()
    push(ss, 6, far, 0, sib)
    fin_copy(yy, 5, far, 1, left).wait_recv()
    push(ss, 7, far, 1, sib)

    outs = []

    def put(slot_t, owner_c, owner_y):
        for n, ref in enumerate((mixed_ref, grad_ref)):
            copy = pltpu.make_async_copy(
                fin.at[slot_t, :, pl.ds(n * half, half)], ref.at[:, columns(owner_c, owner_y)],
                out_sem.at[len(outs)],
            )
            copy.start()
            outs.append(copy)

    for owner_y in (y, left_y, right_y, far_y):
        put(owner_y * 2 + c, c, owner_y)
    for n, (owner_y, h) in enumerate(
        ((y, 0), (y, 1), (left_y, 0), (right_y, 1), (left_y, 1), (right_y, 0), (far_y, 0), (far_y, 1))
    ):
        fin_copy(ss, n, owner_y * 2 + 1 - c, h, sib).wait_recv()
    for owner_y in (y, left_y, right_y, far_y):
        put(owner_y * 2 + 1 - c, 1 - c, owner_y)

    for copy in sends:
        copy.wait_send()

    @pl.loop(0, DIAG)
    def _(j):
        slice_out(j).wait_send()
        far_out(j, right).wait_send()
        near_right(j).wait_send()
        near_left(j).wait_send()
        slice_back(j).wait_send()

    @pl.loop(0, AXIAL)
    def _(j):
        for v in range(RING):
            whole_out(j, v).wait_send()
            whole_back(j, v).wait_send()

    @pl.loop(0, 8)
    def _(i):
        hid_swap(i).wait_send()

    for g in range(3):
        for v in range(RING):
            w_cross(g, v).wait_send()
    for n, v in enumerate((far_y, right_y, left_y)):
        part_sum(n, v).wait_send()
    for copy in outs:
        copy.wait()


def expert_kernel(tokens, cotangent, ids, probs, perm, perm_back, w_gate, w_up, w_down):
    tok, features = tokens.shape
    half = features // (2 * RING)
    width = 2 * half
    dma = pltpu.SemaphoreType.DMA
    vmem = pl.BlockSpec(memory_space=pltpu.VMEM)
    hbm = pl.BlockSpec(memory_space=pltpu.HBM)
    return pl.pallas_call(
        kernel,
        out_shape=[jax.ShapeDtypeStruct((tok, features), BF)] * 2,
        in_specs=[hbm] * 2 + [vmem] * 4 + [hbm] * 3,
        out_specs=[hbm] * 2,
        scratch_shapes=[
            pltpu.VMEM((RING, tok, half), BF),
            pltpu.VMEM((RING, tok, half), BF),
            pltpu.VMEM((tok, tok), F32),
            pltpu.VMEM((tok, tok), F32),
            pltpu.VMEM((AXIAL, ROWS, tok), BF),
            pltpu.VMEM((512, tok), F32),
            pltpu.VMEM((3, 256, tok), F32),
            pltpu.VMEM((3, tok, 512), BF),
            pltpu.VMEM((3, 3, tok, 256), BF),
            pltpu.VMEM((DIAG, 9, SLOTS, width), BF),
            pltpu.VMEM((RING, AXIAL, 9, SLOTS, width), BF),
            pltpu.VMEM((RING, 9, PEERS, SLOTS, width), BF),
            pltpu.VMEM((3, RING, 8, 256, half), BF),
            pltpu.VMEM((144, width), BF),
            pltpu.VMEM((128, width), BF),
            pltpu.VMEM((3, 8, 144, 256), F32),
            pltpu.VMEM((3, 8, 144, 128), F32),
            pltpu.VMEM((3, 8, 144, 256), BF),
            pltpu.VMEM((DIAG, 9, SLOTS, width), BF),
            pltpu.VMEM((2, DIAG, 9, SLOTS, width), BF),
            pltpu.VMEM((DIAG, 9, SLOTS, width), BF),
            pltpu.VMEM((RING, AXIAL + 1, 9, SLOTS, width), BF),
            pltpu.VMEM((tok, width), F32),
            pltpu.VMEM((3, tok, width), BF),
            pltpu.VMEM((3, tok, width), BF),
            pltpu.VMEM((2 * RING, tok, width), BF),
            dma((2, RING)),
            dma((DIAG,)), dma((DIAG,)),
            dma((RING, AXIAL)), dma((RING, AXIAL)),
            dma((2, DIAG)), dma((2, DIAG)),
            dma((DIAG,)), dma((DIAG,)),
            dma((3, RING)), dma((3, RING)), dma((3, RING)),
            dma((8,)), dma((8,)), dma((8,)), dma((8,)),
            dma((DIAG,)), dma((DIAG,)),
            dma((2, DIAG)), dma((2, DIAG)),
            dma((DIAG,)), dma((DIAG,)),
            dma((RING, AXIAL)), dma((RING, AXIAL)),
            dma((3,)), dma((3,)),
            dma((6,)), dma((6,)), dma((8,)), dma((8,)),
            dma((4 * RING,)),
        ],
        compiler_params=pltpu.CompilerParams(
            collective_id=0, has_side_effects=True, vmem_limit_bytes=67_000_000
        ),
    )(tokens, cotangent, ids, probs, perm, perm_back, w_gate, w_up, w_down)


def body(tokens, cotangent, expert_ids, gate_probs, w_gate, w_up, w_down):
    devs = lax.axis_size("expert")
    local_experts = w_gate.shape[0]
    order = jnp.arange(devs * local_experts, dtype=jnp.int32)
    source = (order % devs) * local_experts + order // devs
    perm = (source[:, None] == order[None, :]).astype(BF)
    return tuple(
        expert_kernel(
            tokens, cotangent, expert_ids, gate_probs, perm, perm.T, w_gate, w_up, w_down
        )
    )


def solution(mesh):
    return jax.shard_map(
        body,
        mesh=mesh,
        in_specs=(
            P("expert", None),
            P("expert", None),
            P("expert", None),
            P("expert", None),
            P("expert", "tensor", None),
            P("expert", "tensor", None),
            P("expert", "tensor", None),
        ),
        out_specs=(P("expert", None), P("expert", None)),
        check_vma=False,
    )
```

```python
import jax
import jax.numpy as jnp
from jax import lax
from jax.experimental import pallas as pl
from jax.experimental.pallas import tpu as pltpu
from jax.sharding import PartitionSpec as P

BF = jnp.bfloat16
F32 = jnp.float32
RING = 4
PEERS = 16
SLOTS = 8
AXIAL = 6
DIAG = 9
ROWS = 72
MESH = pl.DeviceIdType.MESH


def flat_rows(block):
    return block.astype(F32).reshape(-1, block.shape[-1]).astype(BF)


def kernel(
    tokens, cotangent, ids_ref, probs_ref, wg, wu, wd,
    mixed_ref, grad_ref,
    tok, cot, perm, perm_back, slot_ref, prob_ref, one_d, wrow_d, wrow_g, coll_d, coll_g,
    sendg, sendd, x, wv, xs, xov, acc, accx, hid, rel, own_in, ret, retd, comb, combs, combr, combf, combh, fin,
    tk, g_s, g_r, d_s, d_r, ag_s, ag_r, rl_s, rl_r, wl, wx_s, wx_r,
    ac_s, ac_r, hd_s, hd_r, h_s, h_r, o_s, o_r, b_s, b_r, rd_s, rd_r, cs_s, cs_r, ch_s, ch_r,
    fy_s, fy_r, fs_s, fs_r, out_sem,
):
    e, t = lax.axis_index("expert"), lax.axis_index("tensor")
    ez, ex = e // RING, e % RING
    y, c = t // 2, t % 2
    right_y, left_y, far_y = (y + 1) % RING, (y + 3) % RING, (y + 2) % RING
    right, left, sib, far = right_y * 2 + c, left_y * 2 + c, y * 2 + 1 - c, far_y * 2 + c
    half = xs.shape[1] // 2
    core_width = half * RING

    def to_of(k):
        return ((ez + k // RING) % RING) * RING + (ex + k % RING) % RING

    def from_of(k):
        return ((ez + RING - k // RING) % RING) * RING + (ex + RING - k % RING) % RING

    def axial(j):
        return (j % 3 + 1) * (1 + 3 * (j // 3))

    def diag(j):
        return (1 + j // 3) * RING + 1 + j % 3

    def remote(src, dst, ssem, rsem, pe, pt):
        return pltpu.make_async_remote_copy(
            src_ref=src, dst_ref=dst, send_sem=ssem, recv_sem=rsem,
            device_id={"expert": pe, "tensor": pt}, device_id_type=MESH,
        )

    def signal(pe, pt):
        pl.semaphore_signal(
            pltpu.get_barrier_semaphore(), inc=1,
            device_id={"expert": pe, "tensor": pt}, device_id_type=MESH,
        )

    mats = (wg, wu, wd)
    hu = wg.shape[1]

    def columns(core, v):
        return pl.ds(pl.multiple_of(core * core_width + v * half, half), half)

    def w_local(g, v):
        return pltpu.make_async_copy(
            mats[g].at[:, :, columns(c, v)], wv.at[g, v, :, pl.ds(0, hu), :], wl.at[g, v]
        )

    def w_cross(g, v):
        return remote(
            mats[g].at[:, :, columns(1 - c, v)], wv.at[g, v, :, pl.ds(128, hu), :],
            wx_s.at[g, v], wx_r.at[g, v], e, sib,
        )

    def t_local(n, v):
        src, dst = ((tokens, tok), (cotangent, cot))[n]
        return pltpu.make_async_copy(src.at[:, columns(c, v)], dst.at[v], tk.at[n, v])

    for v in range(RING):
        for n in range(2):
            t_local(n, v).start()

    @pl.loop(1, PEERS)
    def _(k):
        signal(to_of(k), t)

    for other in (right, left, sib):
        signal(e, other)

    for g in range(3):
        for v in range(RING):
            w_local(g, v).start()

    count = ids_ref.shape[1]
    lane = lax.broadcasted_iota(jnp.int32, (count, count), 1)
    line = lax.broadcasted_iota(jnp.int32, (count, count), 0)
    chosen = jnp.zeros((count, count), F32)
    prob = jnp.zeros((count, count), F32)
    for k in range(ids_ref.shape[0]):
        match = ids_ref[k:k + 1, :] == line
        chosen = chosen + match.astype(F32)
        prob = prob + jnp.where(match, probs_ref[k:k + 1, :], 0.0)
    before = (line < lane).astype(F32).astype(BF)
    slot = jnp.dot(chosen.astype(BF), before, preferred_element_type=F32)
    slot_ref[...] = jnp.where(chosen > 0.5, slot, -1.0)
    prob_ref[...] = prob
    perm[...] = (lane == (line & 15) * SLOTS + (line >> 4)).astype(F32).astype(BF)
    perm_back[...] = (line == (lane & 15) * SLOTS + (lane >> 4)).astype(F32).astype(BF)

    def row_block(j):
        return pl.ds(pl.multiple_of(j * ROWS, SLOTS), ROWS)

    def build(d):
        block = pl.ds(pl.multiple_of(d * SLOTS, SLOTS), SLOTS)
        slots, weights = slot_ref[block, :], prob_ref[block, :]
        number = lax.broadcasted_iota(jnp.int32, (SLOTS, count), 0).astype(F32)
        place, weight = [], []
        for i in range(SLOTS):
            hit = slots[i:i + 1, :] == number
            place.append(hit.astype(F32))
            weight.append(jnp.where(hit, weights[i:i + 1, :], 0.0))
        hit = slots == float(SLOTS)
        place.append(hit.astype(F32))
        weight.append(jnp.where(hit, weights, 0.0))
        return jnp.concatenate(place, axis=0), jnp.concatenate(weight, axis=0)

    def fill(ref, one, weight, v):
        total = jnp.sum(weight, axis=1, keepdims=True)
        rows = jnp.dot(one, tok[v], preferred_element_type=F32)
        ref[:, :, 0:half] = rows.reshape(9, SLOTS, half).astype(BF)
        rows = jnp.dot(one, cot[v], preferred_element_type=F32) * total
        ref[:, :, half:] = rows.reshape(9, SLOTS, half).astype(BF)

    for n in range(2):
        for v in range(RING):
            t_local(n, v).wait()

    @pl.loop(0, DIAG)
    def _(j):
        place, weight = build(to_of(diag(j)))
        wrow_g[j // 3, row_block(j % 3), :] = weight
        fill(sendg.at[j], place.astype(BF), weight, y)

    @pl.loop(0, AXIAL)
    def _(j):
        place, weight = build(to_of(axial(j)))
        wrow_d[row_block(j), :] = weight
        one_d[j] = place.astype(BF)

    pl.semaphore_wait(pltpu.get_barrier_semaphore(), PEERS + 2)

    def slice_out(j):
        return remote(sendg.at[j], x.at[y, :, e], g_s.at[j], g_r.at[j], to_of(diag(j)), t)

    def slice_in(j):
        s = from_of(diag(j))
        return remote(sendg.at[j], x.at[y, :, s], g_s.at[j], g_r.at[j], to_of(diag(j)), t)

    def whole_out(j, v):
        return remote(
            sendd.at[v, j], x.at[v, :, e], d_s.at[v, j], d_r.at[v, j], to_of(axial(j)), t
        )

    def whole_in(j, v):
        s = from_of(axial(j))
        return remote(
            sendd.at[v, j], x.at[v, :, s], d_s.at[v, j], d_r.at[v, j], to_of(axial(j)), t
        )

    @pl.loop(0, DIAG)
    def _(j):
        slice_out(j).start()

    for v in range(RING):
        for g in range(3):
            w_cross(g, v).start()

    def pushed(n, j, dst_y, peer):
        s = from_of(diag(j))
        return remote(x.at[y, :, s], x.at[dst_y, :, s], ag_s.at[n, j], ag_r.at[n, j], e, peer)

    def go_right(j):
        return pushed(0, j, y, right)

    def go_left(j):
        return pushed(1, j, y, left)

    def from_left(j):
        return pushed(0, j, left_y, right)

    def from_right(j):
        return pushed(1, j, right_y, left)

    def relay(j, slice_y, peer):
        s = from_of(diag(j))
        ref = x.at[slice_y, :, s]
        return remote(ref, ref, rl_s.at[j], rl_r.at[j], e, peer)

    @pl.loop(0, DIAG)
    def _(j):
        slice_in(j).wait_recv()
        go_right(j).start()
        go_left(j).start()

        @pl.when(j < DIAG - 1)
        def _():
            for u in range(3):
                n = 3 * j + u
                q, jj = n // AXIAL, n % AXIAL
                v = (y + RING + 2 * q - 1 - 3 * (q // 3) + (3 - q) // 3) % RING
                fill(sendd.at[v, jj], one_d[jj], wrow_d[row_block(jj), :], v)
                whole_out(jj, v).start()

    def relay_even(j):
        from_left(j).wait_recv()
        relay(j, left_y, right).start()
        from_right(j).wait_recv()

    def relay_odd(j):
        from_right(j).wait_recv()
        relay(j, right_y, left).start()
        from_left(j).wait_recv()

    @pl.loop(0, DIAG // 2)
    def _(j):
        relay_even(2 * j)
        relay_odd(2 * j + 1)

    relay_even(DIAG - 1)

    place, weight = build(e)
    wrow_d[row_block(AXIAL), :] = weight
    place = place.astype(BF)
    for v in range(RING):
        fill(x.at[v, :, e], place, weight, v)

    zeros = jnp.zeros((8, 16, half), BF)
    for g in range(3):
        for v in range(RING):
            wv[g, v, :, hu:128, :] = zeros
            wv[g, v, :, 128 + hu:256, :] = zeros

    for v in range(RING):
        for g in range(3):
            w_local(g, v).wait()
            w_cross(g, v).wait_recv()

    def acc_swap(i):
        return remote(
            acc.at[:, i, :, pl.ds(128, 128)], accx.at[:, i], ac_s.at[i], ac_r.at[i], e, sib
        )

    def hid_swap(i):
        return remote(
            hid.at[:, i, :, pl.ds(0, 128)], hid.at[:, i, :, pl.ds(128, 128)],
            hd_s.at[i], hd_r.at[i], e, sib,
        )

    def activate(i):
        acc_swap(i).wait()
        pre = acc[0, i, :, 0:128] + accx[0, i]
        up = acc[1, i, :, 0:128] + accx[1, i]
        gh = acc[2, i, :, 0:128] + accx[2, i]
        sg = jax.nn.sigmoid(pre)
        act = pre * sg
        hid[0, i, :, 0:128] = (act * up).astype(BF)
        hid[1, i, :, 0:128] = (gh * up * sg * (1.0 + pre * (1.0 - sg))).astype(BF)
        hid[2, i, :, 0:128] = (gh * act).astype(BF)
        hid_swap(i).start()

    def contract(v, start, end):
        @pl.loop(0, AXIAL)
        def _(j):
            whole_in(j, v).wait_recv()

        xov[...] = jnp.dot(perm[...], flat_rows(x[v, 8]), preferred_element_type=F32).astype(BF)

        @pl.loop(0, 8)
        def _(i):
            xs[0:128, :] = flat_rows(x[v, i])
            xs[128:144, :] = xov[pl.ds(pl.multiple_of(i * 16, 16), 16), :]
            for g in range(3):
                rows = xs[:, 0:half] if g < 2 else xs[:, half:]
                part = lax.dot_general(
                    rows, wv[g, v, i], (((1,), (1,)), ((), ())), preferred_element_type=F32
                )
                if start:
                    acc[g, i] = part
                else:
                    acc[g, i] = acc[g, i] + part
            if end:
                acc_swap(i).start()

                @pl.when(i >= 2)
                def _():
                    activate(i - 2)

        if end:
            activate(6)
            activate(7)

    contract(y, True, False)
    contract(right_y, False, False)
    contract(left_y, False, False)

    @pl.loop(0, DIAG)
    def _(j):
        relay(j, far_y, right).wait_recv()

    contract(far_y, False, True)

    @pl.loop(0, DIAG)
    def _(j):
        go_right(j).wait_send()
        go_left(j).wait_send()
        relay(j, left_y, right).wait_send()

    def whole_back(j, v):
        s = from_of(axial(j))
        return remote(x.at[v, :, s], retd.at[v, j], rd_s.at[v, j], rd_r.at[v, j], s, t)

    def expand(v, start=False):
        @pl.loop(0, 8)
        def _(i):
            if start:
                hid_swap(i).wait_recv()
            out = jnp.dot(hid[0, i], wv[2, v, i], preferred_element_type=F32)
            x[v, i, :, :, 0:half] = out[0:128].reshape(PEERS, SLOTS, half).astype(BF)
            tail = pl.ds(pl.multiple_of(i * 16, 16), 16)
            xov[tail, 0:half] = out[128:144].astype(BF)
            grad = jnp.dot(hid[1, i], wv[0, v, i], preferred_element_type=F32)
            grad = grad + jnp.dot(hid[2, i], wv[1, v, i], preferred_element_type=F32)
            x[v, i, :, :, half:] = grad[0:128].reshape(PEERS, SLOTS, half).astype(BF)
            xov[tail, half:] = grad[128:144].astype(BF)

        over = jnp.dot(perm_back[...], xov[...], preferred_element_type=F32)
        x[v, 8] = over.reshape(PEERS, SLOTS, 2 * half).astype(BF)

    def return_whole(v):
        @pl.loop(0, AXIAL)
        def _(j):
            whole_back(j, v).start()

    def far_out(j, peer):
        s = from_of(diag(j))
        return remote(x.at[far_y, :, s], rel.at[j], h_s.at[j], h_r.at[j], e, peer)

    def near(n, j, slice_y, peer):
        s = from_of(diag(j))
        return remote(x.at[slice_y, :, s], own_in.at[n, j], o_s.at[n, j], o_r.at[n, j], e, peer)

    def near_right(j):
        return near(0, j, right_y, right)

    def near_left(j):
        return near(1, j, left_y, left)

    def add_relayed(j, slice_y):
        far_out(j, right).wait_recv()
        s = from_of(diag(j))
        x[slice_y, :, s] = (x[slice_y, :, s].astype(F32) + rel[j].astype(F32)).astype(BF)

    expand(far_y, True)

    @pl.loop(0, DIAG // 2)
    def _(j):
        far_out(2 * j, right).start()
        far_out(2 * j + 1, left).start()

    far_out(DIAG - 1, right).start()
    return_whole(far_y)
    expand(right_y)
    near_right(1).start()
    return_whole(right_y)
    expand(left_y)
    near_left(0).start()
    return_whole(left_y)
    expand(y)
    return_whole(y)

    def split(ref, weights):
        weights = weights.T
        hi = weights.astype(BF)
        ref[0] = hi
        ref[1] = (weights - hi.astype(F32)).astype(BF)
        ref[2] = (weights > 0.0).astype(F32).astype(BF)

    def gathered(coll, rows):
        width = rows.shape[0]
        low = rows[:, 0:half]
        part = jnp.dot(coll[0, :, 0:width], low, preferred_element_type=F32)
        part = part + jnp.dot(coll[1, :, 0:width], low, preferred_element_type=F32)
        return part, jnp.dot(coll[2, :, 0:width], rows[:, half:], preferred_element_type=F32)

    wrow_d[(AXIAL + 1) * ROWS:, :] = jnp.zeros((wrow_d.shape[0] - (AXIAL + 1) * ROWS, count), F32)
    split(coll_d, wrow_d[...])
    for n in range(3):
        wrow_g[n, 3 * ROWS:, :] = jnp.zeros((wrow_g.shape[1] - 3 * ROWS, count), F32)
        split(coll_g.at[n], wrow_g[n])

    def whole_sum(v):
        retd[v, AXIAL] = x[v, :, e]

        @pl.loop(0, AXIAL)
        def _(j):
            whole_back(j, v).wait_recv()

        return gathered(coll_d, flat_rows(retd[v]))

    def part_sum(n, peer):
        return remote(combs.at[n], combr.at[n], cs_s.at[n], cs_r.at[n], e, peer)

    def part_half(n, peer):
        return remote(combf.at[n], combh.at[n], ch_s.at[n], ch_r.at[n], e, peer)

    m, g = whole_sum(far_y)
    combf[0] = m.astype(BF)
    combf[1] = g.astype(BF)
    part_half(0, right).start()
    part_half(1, left).start()

    @pl.loop(0, DIAG // 2)
    def _(j):
        even, odd = 2 * j, 2 * j + 1
        add_relayed(even, right_y)
        near_right(even).start()
        near_left(even + 2).start()
        add_relayed(odd, left_y)
        near_left(odd).start()

        @pl.when(j < DIAG // 2 - 1)
        def _():
            near_right(odd + 2).start()

    add_relayed(DIAG - 1, right_y)
    near_right(DIAG - 1).start()

    m, g = whole_sum(right_y)
    part_half(0, right).wait_recv()
    combs[0, :, 0:half] = (m + combh[0].astype(F32)).astype(BF)
    combs[0, :, half:] = g.astype(BF)
    part_sum(0, right).start()
    m, g = whole_sum(left_y)
    part_half(1, left).wait_recv()
    combs[1, :, 0:half] = m.astype(BF)
    combs[1, :, half:] = (g + combh[1].astype(F32)).astype(BF)
    part_sum(1, left).start()
    comb[:, 0:half], comb[:, half:] = whole_sum(y)

    def slice_back(j):
        s = from_of(diag(j))
        return remote(x.at[y, :, s], ret.at[j], b_s.at[j], b_r.at[j], s, t)

    @pl.loop(0, DIAG)
    def _(j):
        near_right(j).wait_recv()
        near_left(j).wait_recv()
        s = from_of(diag(j))
        total = x[y, :, s].astype(F32) + own_in[0, j].astype(F32)
        x[y, :, s] = (total + own_in[1, j].astype(F32)).astype(BF)
        slice_back(j).start()

    for n, peer in enumerate((right, left)):
        part_sum(n, peer).wait_recv()
        comb[...] = comb[...] + combr[n].astype(F32)
    for n in range(3):
        for j in range(3 * n, 3 * n + 3):
            slice_back(j).wait_recv()
        m, g = gathered(coll_g.at[n], flat_rows(ret[3 * n:3 * n + 3]))
        comb[:, 0:half] = comb[:, 0:half] + m
        comb[:, half:] = comb[:, half:] + g
    fin[t] = comb[...].astype(BF)

    rows_of = (pl.ds(0, 64), pl.ds(64, 64))

    def fin_copy(sems, n, slot_t, h, peer):
        ref = fin.at[slot_t, rows_of[h], :]
        return remote(ref, ref, sems[0].at[n], sems[1].at[n], e, peer)

    yy, ss = (fy_s, fy_r), (fs_s, fs_r)
    sends = []

    def push(sems, n, slot_t, h, peer):
        copy = fin_copy(sems, n, slot_t, h, peer)
        copy.start()
        sends.append(copy)

    push(yy, 0, t, 0, right)
    push(yy, 1, t, 1, left)
    push(yy, 2, t, 1, right)
    push(yy, 3, t, 0, left)
    push(ss, 0, t, 0, sib)
    push(ss, 1, t, 1, sib)
    fin_copy(yy, 0, left, 0, right).wait_recv()
    push(yy, 4, left, 0, right)
    push(ss, 2, left, 0, sib)
    fin_copy(yy, 1, right, 1, left).wait_recv()
    push(yy, 5, right, 1, left)
    push(ss, 3, right, 1, sib)
    fin_copy(yy, 2, left, 1, right).wait_recv()
    push(ss, 4, left, 1, sib)
    fin_copy(yy, 3, right, 0, left).wait_recv()
    push(ss, 5, right, 0, sib)
    fin_copy(yy, 4, far, 0, right).wait_recv()
    push(ss, 6, far, 0, sib)
    fin_copy(yy, 5, far, 1, left).wait_recv()
    push(ss, 7, far, 1, sib)

    outs = []

    def put(slot_t, owner_c, owner_y):
        for n, ref in enumerate((mixed_ref, grad_ref)):
            copy = pltpu.make_async_copy(
                fin.at[slot_t, :, pl.ds(n * half, half)], ref.at[:, columns(owner_c, owner_y)],
                out_sem.at[len(outs)],
            )
            copy.start()
            outs.append(copy)

    for owner_y in (y, left_y, right_y, far_y):
        put(owner_y * 2 + c, c, owner_y)
    for n, (owner_y, h) in enumerate(
        ((y, 0), (y, 1), (left_y, 0), (right_y, 1), (left_y, 1), (right_y, 0), (far_y, 0), (far_y, 1))
    ):
        fin_copy(ss, n, owner_y * 2 + 1 - c, h, sib).wait_recv()
    for owner_y in (y, left_y, right_y, far_y):
        put(owner_y * 2 + 1 - c, 1 - c, owner_y)

    for copy in sends:
        copy.wait_send()

    @pl.loop(0, DIAG)
    def _(j):
        slice_out(j).wait_send()
        far_out(j, right).wait_send()
        near_right(j).wait_send()
        near_left(j).wait_send()
        slice_back(j).wait_send()

    @pl.loop(0, AXIAL)
    def _(j):
        for v in range(RING):
            whole_out(j, v).wait_send()
            whole_back(j, v).wait_send()

    @pl.loop(0, 8)
    def _(i):
        hid_swap(i).wait_send()

    for g in range(3):
        for v in range(RING):
            w_cross(g, v).wait_send()
    for n, peer in enumerate((right, left)):
        part_sum(n, peer).wait_send()
        part_half(n, peer).wait_send()
    for copy in outs:
        copy.wait()


def expert_kernel(tokens, cotangent, ids, probs, w_gate, w_up, w_down):
    tok, features = tokens.shape
    half = features // (2 * RING)
    width = 2 * half
    dma = pltpu.SemaphoreType.DMA
    vmem = pl.BlockSpec(memory_space=pltpu.VMEM)
    hbm = pl.BlockSpec(memory_space=pltpu.HBM)
    return pl.pallas_call(
        kernel,
        out_shape=[jax.ShapeDtypeStruct((tok, features), BF)] * 2,
        in_specs=[hbm] * 2 + [vmem] * 2 + [hbm] * 3,
        out_specs=[hbm] * 2,
        scratch_shapes=[
            pltpu.VMEM((RING, tok, half), BF),
            pltpu.VMEM((RING, tok, half), BF),
            pltpu.VMEM((tok, tok), BF),
            pltpu.VMEM((tok, tok), BF),
            pltpu.VMEM((tok, tok), F32),
            pltpu.VMEM((tok, tok), F32),
            pltpu.VMEM((AXIAL, ROWS, tok), BF),
            pltpu.VMEM((512, tok), F32),
            pltpu.VMEM((3, 256, tok), F32),
            pltpu.VMEM((3, tok, 512), BF),
            pltpu.VMEM((3, 3, tok, 256), BF),
            pltpu.VMEM((DIAG, 9, SLOTS, width), BF),
            pltpu.VMEM((RING, AXIAL, 9, SLOTS, width), BF),
            pltpu.VMEM((RING, 9, PEERS, SLOTS, width), BF),
            pltpu.VMEM((3, RING, 8, 256, half), BF),
            pltpu.VMEM((144, width), BF),
            pltpu.VMEM((128, width), BF),
            pltpu.VMEM((3, 8, 144, 256), F32),
            pltpu.VMEM((3, 8, 144, 128), F32),
            pltpu.VMEM((3, 8, 144, 256), BF),
            pltpu.VMEM((DIAG, 9, SLOTS, width), BF),
            pltpu.VMEM((2, DIAG, 9, SLOTS, width), BF),
            pltpu.VMEM((DIAG, 9, SLOTS, width), BF),
            pltpu.VMEM((RING, AXIAL + 1, 9, SLOTS, width), BF),
            pltpu.VMEM((tok, width), F32),
            pltpu.VMEM((2, tok, width), BF),
            pltpu.VMEM((2, tok, width), BF),
            pltpu.VMEM((2, tok, half), BF),
            pltpu.VMEM((2, tok, half), BF),
            pltpu.VMEM((2 * RING, tok, width), BF),
            dma((2, RING)),
            dma((DIAG,)), dma((DIAG,)),
            dma((RING, AXIAL)), dma((RING, AXIAL)),
            dma((2, DIAG)), dma((2, DIAG)),
            dma((DIAG,)), dma((DIAG,)),
            dma((3, RING)), dma((3, RING)), dma((3, RING)),
            dma((8,)), dma((8,)), dma((8,)), dma((8,)),
            dma((DIAG,)), dma((DIAG,)),
            dma((2, DIAG)), dma((2, DIAG)),
            dma((DIAG,)), dma((DIAG,)),
            dma((RING, AXIAL)), dma((RING, AXIAL)),
            dma((2,)), dma((2,)), dma((2,)), dma((2,)),
            dma((6,)), dma((6,)), dma((8,)), dma((8,)),
            dma((4 * RING,)),
        ],
        compiler_params=pltpu.CompilerParams(
            collective_id=0, has_side_effects=True, vmem_limit_bytes=67_000_000
        ),
    )(tokens, cotangent, ids, probs, w_gate, w_up, w_down)


def body(tokens, cotangent, expert_ids, gate_probs, w_gate, w_up, w_down):
    return tuple(
        expert_kernel(
            tokens, cotangent, expert_ids.T, gate_probs.T, w_gate, w_up, w_down
        )
    )


def solution(mesh):
    return jax.shard_map(
        body,
        mesh=mesh,
        in_specs=(
            P("expert", None),
            P("expert", None),
            P("expert", None),
            P("expert", None),
            P("expert", "tensor", None),
            P("expert", "tensor", None),
            P("expert", "tensor", None),
        ),
        out_specs=(P("expert", None), P("expert", None)),
        check_vma=False,
    )
```

```python
import jax
import jax.numpy as jnp
from jax import lax
from jax.experimental import pallas as pl
from jax.experimental.pallas import tpu as pltpu
from jax.sharding import PartitionSpec as P

BF = jnp.bfloat16
F32 = jnp.float32
RING = 4
PEERS = 16
SLOTS = 8
AXIAL = 6
DIAG = 9
ROWS = 72
MESH = pl.DeviceIdType.MESH


def flat_rows(block):
    return block.astype(F32).reshape(-1, block.shape[-1]).astype(BF)


def kernel(
    tokens, cotangent, ids_ref, probs_ref, wg, wu, wd,
    mixed_ref, grad_ref,
    tok, cot, perm, perm_back, slot_ref, prob_ref, one_d, wrow_d, wrow_g, coll_d, coll_g,
    sendg, sendd, x, wv, xs, xov, acc, accx, hid, rel, own_in, ret, retd, comb, combs, combr, combf, combh, fin,
    tk, g_s, g_r, d_s, d_r, ag_s, ag_r, rl_s, rl_r, wl, wx_s, wx_r,
    ac_s, ac_r, hd_s, hd_r, h_s, h_r, o_s, o_r, b_s, b_r, rd_s, rd_r, cs_s, cs_r, ch_s, ch_r,
    fy_s, fy_r, fs_s, fs_r, out_sem,
):
    e, t = lax.axis_index("expert"), lax.axis_index("tensor")
    ez, ex = e // RING, e % RING
    y, c = t // 2, t % 2
    right_y, left_y, far_y = (y + 1) % RING, (y + 3) % RING, (y + 2) % RING
    right, left, sib, far = right_y * 2 + c, left_y * 2 + c, y * 2 + 1 - c, far_y * 2 + c
    half = xs.shape[1] // 2
    core_width = half * RING

    def to_of(k):
        return ((ez + k // RING) % RING) * RING + (ex + k % RING) % RING

    def from_of(k):
        return ((ez + RING - k // RING) % RING) * RING + (ex + RING - k % RING) % RING

    def axial(j):
        return (1 + 2 * (j // 2) - 3 * (j // 4)) * (1 + 3 * (j % 2))

    def diag(j):
        place = (4 * j) % DIAG
        return (1 + place // 3) * RING + 1 + place % 3

    def remote(src, dst, ssem, rsem, pe, pt):
        return pltpu.make_async_remote_copy(
            src_ref=src, dst_ref=dst, send_sem=ssem, recv_sem=rsem,
            device_id={"expert": pe, "tensor": pt}, device_id_type=MESH,
        )

    def signal(pe, pt):
        pl.semaphore_signal(
            pltpu.get_barrier_semaphore(), inc=1,
            device_id={"expert": pe, "tensor": pt}, device_id_type=MESH,
        )

    mats = (wg, wu, wd)
    hu = wg.shape[1]

    def columns(core, v):
        return pl.ds(pl.multiple_of(core * core_width + v * half, half), half)

    def w_local(g, v):
        return pltpu.make_async_copy(
            mats[g].at[:, :, columns(c, v)], wv.at[g, v, :, pl.ds(0, hu), :], wl.at[g, v]
        )

    def w_cross(g, v):
        return remote(
            mats[g].at[:, :, columns(1 - c, v)], wv.at[g, v, :, pl.ds(128, hu), :],
            wx_s.at[g, v], wx_r.at[g, v], e, sib,
        )

    def t_local(n, v):
        src, dst = ((tokens, tok), (cotangent, cot))[n]
        return pltpu.make_async_copy(src.at[:, columns(c, v)], dst.at[v], tk.at[n, v])

    for v in range(RING):
        for n in range(2):
            t_local(n, v).start()

    @pl.loop(1, PEERS)
    def _(k):
        signal(to_of(k), t)

    for other in (right, left, sib):
        signal(e, other)

    for g in range(3):
        for v in range(RING):
            w_local(g, v).start()

    count = ids_ref.shape[1]
    lane = lax.broadcasted_iota(jnp.int32, (count, count), 1)
    line = lax.broadcasted_iota(jnp.int32, (count, count), 0)
    chosen = jnp.zeros((count, count), F32)
    prob = jnp.zeros((count, count), F32)
    for k in range(ids_ref.shape[0]):
        match = ids_ref[k:k + 1, :] == line
        chosen = chosen + match.astype(F32)
        prob = prob + jnp.where(match, probs_ref[k:k + 1, :], 0.0)
    before = (line < lane).astype(F32).astype(BF)
    slot = jnp.dot(chosen.astype(BF), before, preferred_element_type=F32)
    slot_ref[...] = jnp.where(chosen > 0.5, slot, -1.0)
    prob_ref[...] = prob
    perm[...] = (lane == (line & 15) * SLOTS + (line >> 4)).astype(F32).astype(BF)
    perm_back[...] = (line == (lane & 15) * SLOTS + (lane >> 4)).astype(F32).astype(BF)

    def row_block(j):
        return pl.ds(pl.multiple_of(j * ROWS, SLOTS), ROWS)

    def build(d):
        block = pl.ds(pl.multiple_of(d * SLOTS, SLOTS), SLOTS)
        slots, weights = slot_ref[block, :], prob_ref[block, :]
        number = lax.broadcasted_iota(jnp.int32, (SLOTS, count), 0).astype(F32)
        place, weight = [], []
        for i in range(SLOTS):
            hit = slots[i:i + 1, :] == number
            place.append(hit.astype(F32))
            weight.append(jnp.where(hit, weights[i:i + 1, :], 0.0))
        hit = slots == float(SLOTS)
        place.append(hit.astype(F32))
        weight.append(jnp.where(hit, weights, 0.0))
        return jnp.concatenate(place, axis=0), jnp.concatenate(weight, axis=0)

    def fill(ref, one, weight, v):
        total = jnp.sum(weight, axis=1, keepdims=True)
        rows = jnp.dot(one, tok[v], preferred_element_type=F32)
        ref[:, :, 0:half] = rows.reshape(9, SLOTS, half).astype(BF)
        rows = jnp.dot(one, cot[v], preferred_element_type=F32) * total
        ref[:, :, half:] = rows.reshape(9, SLOTS, half).astype(BF)

    for n in range(2):
        for v in range(RING):
            t_local(n, v).wait()

    @pl.loop(0, DIAG)
    def _(j):
        place, weight = build(to_of(diag(j)))
        wrow_g[j // 3, row_block(j % 3), :] = weight
        fill(sendg.at[j], place.astype(BF), weight, y)

    @pl.loop(0, AXIAL)
    def _(j):
        place, weight = build(to_of(axial(j)))
        wrow_d[row_block(j), :] = weight
        one_d[j] = place.astype(BF)

    pl.semaphore_wait(pltpu.get_barrier_semaphore(), PEERS + 2)

    def slice_out(j):
        return remote(sendg.at[j], x.at[y, :, e], g_s.at[j], g_r.at[j], to_of(diag(j)), t)

    def slice_in(j):
        s = from_of(diag(j))
        return remote(sendg.at[j], x.at[y, :, s], g_s.at[j], g_r.at[j], to_of(diag(j)), t)

    def whole_out(j, v):
        return remote(
            sendd.at[v, j], x.at[v, :, e], d_s.at[v, j], d_r.at[v, j], to_of(axial(j)), t
        )

    def whole_in(j, v):
        s = from_of(axial(j))
        return remote(
            sendd.at[v, j], x.at[v, :, s], d_s.at[v, j], d_r.at[v, j], to_of(axial(j)), t
        )

    @pl.loop(0, DIAG)
    def _(j):
        slice_out(j).start()

    for v in range(RING):
        for g in range(3):
            w_cross(g, v).start()

    def turn(q):
        return (y + RING + 2 * q - 1 - 3 * (q // 3) + (3 - q) // 3) % RING

    def pushed(n, j, dst_y, peer):
        s = from_of(diag(j))
        return remote(x.at[y, :, s], x.at[dst_y, :, s], ag_s.at[n, j], ag_r.at[n, j], e, peer)

    def go_right(j):
        return pushed(0, j, y, right)

    def go_left(j):
        return pushed(1, j, y, left)

    def from_left(j):
        return pushed(0, j, left_y, right)

    def from_right(j):
        return pushed(1, j, right_y, left)

    def relay(j, slice_y, peer):
        s = from_of(diag(j))
        ref = x.at[slice_y, :, s]
        return remote(ref, ref, rl_s.at[j], rl_r.at[j], e, peer)

    @pl.loop(0, DIAG)
    def _(j):
        slice_in(j).wait_recv()
        go_right(j).start()
        go_left(j).start()

        @pl.when(j < DIAG - 1)
        def _():
            for u in range(3):
                n = 3 * j + u
                v, jj = turn(n // AXIAL), n % AXIAL
                fill(sendd.at[v, jj], one_d[jj], wrow_d[row_block(jj), :], v)

        @pl.when((j >= 5) & (j < 9))
        def _():
            v = turn(j - 5)

            @pl.loop(0, AXIAL)
            def _(jj):
                whole_out(jj, v).start()

    def relay_even(j):
        from_left(j).wait_recv()
        relay(j, left_y, right).start()
        from_right(j).wait_recv()

    def relay_odd(j):
        from_right(j).wait_recv()
        relay(j, right_y, left).start()
        from_left(j).wait_recv()

    @pl.loop(0, DIAG // 2)
    def _(j):
        relay_even(2 * j)
        relay_odd(2 * j + 1)

    relay_even(DIAG - 1)

    place, weight = build(e)
    wrow_d[row_block(AXIAL), :] = weight
    place = place.astype(BF)
    for v in range(RING):
        fill(x.at[v, :, e], place, weight, v)

    zeros = jnp.zeros((8, 16, half), BF)
    for g in range(3):
        for v in range(RING):
            wv[g, v, :, hu:128, :] = zeros
            wv[g, v, :, 128 + hu:256, :] = zeros

    for v in range(RING):
        for g in range(3):
            w_local(g, v).wait()
            w_cross(g, v).wait_recv()

    def acc_swap(i):
        return remote(
            acc.at[:, i, :, pl.ds(128, 128)], accx.at[:, i], ac_s.at[i], ac_r.at[i], e, sib
        )

    def hid_swap(i):
        return remote(
            hid.at[:, i, :, pl.ds(0, 128)], hid.at[:, i, :, pl.ds(128, 128)],
            hd_s.at[i], hd_r.at[i], e, sib,
        )

    def activate(i):
        acc_swap(i).wait()
        pre = acc[0, i, :, 0:128] + accx[0, i]
        up = acc[1, i, :, 0:128] + accx[1, i]
        gh = acc[2, i, :, 0:128] + accx[2, i]
        sg = jax.nn.sigmoid(pre)
        act = pre * sg
        hid[0, i, :, 0:128] = (act * up).astype(BF)
        hid[1, i, :, 0:128] = (gh * up * sg * (1.0 + pre * (1.0 - sg))).astype(BF)
        hid[2, i, :, 0:128] = (gh * act).astype(BF)
        hid_swap(i).start()

    def contract(v, start, end):
        @pl.loop(0, AXIAL)
        def _(j):
            whole_in(j, v).wait_recv()

        xov[...] = jnp.dot(perm[...], flat_rows(x[v, 8]), preferred_element_type=F32).astype(BF)

        @pl.loop(0, 8)
        def _(i):
            xs[0:128, :] = flat_rows(x[v, i])
            xs[128:144, :] = xov[pl.ds(pl.multiple_of(i * 16, 16), 16), :]
            for g in range(3):
                rows = xs[:, 0:half] if g < 2 else xs[:, half:]
                part = lax.dot_general(
                    rows, wv[g, v, i], (((1,), (1,)), ((), ())), preferred_element_type=F32
                )
                if start:
                    acc[g, i] = part
                else:
                    acc[g, i] = acc[g, i] + part
            if end:
                acc_swap(i).start()

                @pl.when(i >= 2)
                def _():
                    activate(i - 2)

        if end:
            activate(6)
            activate(7)

    contract(y, True, False)
    contract(right_y, False, False)
    contract(left_y, False, False)

    @pl.loop(0, DIAG)
    def _(j):
        relay(j, far_y, right).wait_recv()

    contract(far_y, False, True)

    @pl.loop(0, DIAG)
    def _(j):
        go_right(j).wait_send()
        go_left(j).wait_send()
        relay(j, left_y, right).wait_send()

    def whole_back(j, v):
        s = from_of(axial(j))
        return remote(x.at[v, :, s], retd.at[v, j], rd_s.at[v, j], rd_r.at[v, j], s, t)

    def expand(v, start=False):
        @pl.loop(0, 8)
        def _(i):
            if start:
                hid_swap(i).wait_recv()
            out = jnp.dot(hid[0, i], wv[2, v, i], preferred_element_type=F32)
            x[v, i, :, :, 0:half] = out[0:128].reshape(PEERS, SLOTS, half).astype(BF)
            tail = pl.ds(pl.multiple_of(i * 16, 16), 16)
            xov[tail, 0:half] = out[128:144].astype(BF)
            grad = jnp.dot(hid[1, i], wv[0, v, i], preferred_element_type=F32)
            grad = grad + jnp.dot(hid[2, i], wv[1, v, i], preferred_element_type=F32)
            x[v, i, :, :, half:] = grad[0:128].reshape(PEERS, SLOTS, half).astype(BF)
            xov[tail, half:] = grad[128:144].astype(BF)

        over = jnp.dot(perm_back[...], xov[...], preferred_element_type=F32)
        x[v, 8] = over.reshape(PEERS, SLOTS, 2 * half).astype(BF)

    def return_whole(v):
        @pl.loop(0, AXIAL)
        def _(j):
            whole_back(j, v).start()

    def far_out(j, peer):
        s = from_of(diag(j))
        return remote(x.at[far_y, :, s], rel.at[j], h_s.at[j], h_r.at[j], e, peer)

    def near(n, j, slice_y, peer):
        s = from_of(diag(j))
        return remote(x.at[slice_y, :, s], own_in.at[n, j], o_s.at[n, j], o_r.at[n, j], e, peer)

    def near_right(j):
        return near(0, j, right_y, right)

    def near_left(j):
        return near(1, j, left_y, left)

    def add_relayed(j, slice_y):
        far_out(j, right).wait_recv()
        s = from_of(diag(j))
        x[slice_y, :, s] = (x[slice_y, :, s].astype(F32) + rel[j].astype(F32)).astype(BF)

    expand(far_y, True)

    @pl.loop(0, DIAG // 2)
    def _(j):
        far_out(2 * j, right).start()
        far_out(2 * j + 1, left).start()

    far_out(DIAG - 1, right).start()
    return_whole(far_y)
    expand(right_y)
    near_right(1).start()
    return_whole(right_y)
    expand(left_y)
    near_left(0).start()
    return_whole(left_y)
    expand(y)
    return_whole(y)

    def split(ref, weights):
        weights = weights.T
        hi = weights.astype(BF)
        ref[0] = hi
        ref[1] = (weights - hi.astype(F32)).astype(BF)
        ref[2] = (weights > 0.0).astype(F32).astype(BF)

    def gathered(coll, rows):
        width = rows.shape[0]
        low = rows[:, 0:half]
        part = jnp.dot(coll[0, :, 0:width], low, preferred_element_type=F32)
        part = part + jnp.dot(coll[1, :, 0:width], low, preferred_element_type=F32)
        return part, jnp.dot(coll[2, :, 0:width], rows[:, half:], preferred_element_type=F32)

    wrow_d[(AXIAL + 1) * ROWS:, :] = jnp.zeros((wrow_d.shape[0] - (AXIAL + 1) * ROWS, count), F32)
    split(coll_d, wrow_d[...])
    for n in range(3):
        wrow_g[n, 3 * ROWS:, :] = jnp.zeros((wrow_g.shape[1] - 3 * ROWS, count), F32)
        split(coll_g.at[n], wrow_g[n])

    def whole_sum(v):
        retd[v, AXIAL] = x[v, :, e]

        @pl.loop(0, AXIAL)
        def _(j):
            whole_back(j, v).wait_recv()

        return gathered(coll_d, flat_rows(retd[v]))

    def part_sum(n, peer):
        return remote(combs.at[n], combr.at[n], cs_s.at[n], cs_r.at[n], e, peer)

    def part_half(n, peer):
        return remote(combf.at[n], combh.at[n], ch_s.at[n], ch_r.at[n], e, peer)

    m, g = whole_sum(far_y)
    combf[0] = m.astype(BF)
    combf[1] = g.astype(BF)
    part_half(0, right).start()
    part_half(1, left).start()

    @pl.loop(0, DIAG // 2)
    def _(j):
        even, odd = 2 * j, 2 * j + 1
        add_relayed(even, right_y)
        near_right(even).start()
        near_left(even + 2).start()
        add_relayed(odd, left_y)
        near_left(odd).start()

        @pl.when(j < DIAG // 2 - 1)
        def _():
            near_right(odd + 2).start()

    add_relayed(DIAG - 1, right_y)
    near_right(DIAG - 1).start()

    m, g = whole_sum(right_y)
    part_half(0, right).wait_recv()
    combs[0, :, 0:half] = (m + combh[0].astype(F32)).astype(BF)
    combs[0, :, half:] = g.astype(BF)
    part_sum(0, right).start()
    m, g = whole_sum(left_y)
    part_half(1, left).wait_recv()
    combs[1, :, 0:half] = m.astype(BF)
    combs[1, :, half:] = (g + combh[1].astype(F32)).astype(BF)
    part_sum(1, left).start()
    def slice_back(j):
        s = from_of(diag(j))
        return remote(x.at[y, :, s], ret.at[j], b_s.at[j], b_r.at[j], s, t)

    @pl.loop(0, DIAG)
    def _(j):
        near_right(j).wait_recv()
        near_left(j).wait_recv()
        s = from_of(diag(j))
        total = x[y, :, s].astype(F32) + own_in[0, j].astype(F32)
        x[y, :, s] = (total + own_in[1, j].astype(F32)).astype(BF)
        slice_back(j).start()

    comb[:, 0:half], comb[:, half:] = whole_sum(y)
    for n, peer in enumerate((right, left)):
        part_sum(n, peer).wait_recv()
        comb[...] = comb[...] + combr[n].astype(F32)
    for n in range(3):
        for j in range(3 * n, 3 * n + 3):
            slice_back(j).wait_recv()
        m, g = gathered(coll_g.at[n], flat_rows(ret[3 * n:3 * n + 3]))
        comb[:, 0:half] = comb[:, 0:half] + m
        comb[:, half:] = comb[:, half:] + g
    fin[t] = comb[...].astype(BF)

    rows_of = (pl.ds(0, 64), pl.ds(64, 64))

    def fin_copy(sems, n, slot_t, h, peer):
        ref = fin.at[slot_t, rows_of[h], :]
        return remote(ref, ref, sems[0].at[n], sems[1].at[n], e, peer)

    yy, ss = (fy_s, fy_r), (fs_s, fs_r)
    sends = []

    def push(sems, n, slot_t, h, peer):
        copy = fin_copy(sems, n, slot_t, h, peer)
        copy.start()
        sends.append(copy)

    push(yy, 0, t, 0, right)
    push(yy, 1, t, 1, left)
    push(yy, 2, t, 1, right)
    push(yy, 3, t, 0, left)
    push(ss, 0, t, 0, sib)
    push(ss, 1, t, 1, sib)
    fin_copy(yy, 0, left, 0, right).wait_recv()
    push(yy, 4, left, 0, right)
    push(ss, 2, left, 0, sib)
    fin_copy(yy, 1, right, 1, left).wait_recv()
    push(yy, 5, right, 1, left)
    push(ss, 3, right, 1, sib)
    fin_copy(yy, 2, left, 1, right).wait_recv()
    push(ss, 4, left, 1, sib)
    fin_copy(yy, 3, right, 0, left).wait_recv()
    push(ss, 5, right, 0, sib)
    fin_copy(yy, 4, far, 0, right).wait_recv()
    push(ss, 6, far, 0, sib)
    fin_copy(yy, 5, far, 1, left).wait_recv()
    push(ss, 7, far, 1, sib)

    outs = []

    def put(slot_t, owner_c, owner_y):
        for n, ref in enumerate((mixed_ref, grad_ref)):
            copy = pltpu.make_async_copy(
                fin.at[slot_t, :, pl.ds(n * half, half)], ref.at[:, columns(owner_c, owner_y)],
                out_sem.at[len(outs)],
            )
            copy.start()
            outs.append(copy)

    for owner_y in (y, left_y, right_y, far_y):
        put(owner_y * 2 + c, c, owner_y)
    for n, (owner_y, h) in enumerate(
        ((y, 0), (y, 1), (left_y, 0), (right_y, 1), (left_y, 1), (right_y, 0), (far_y, 0), (far_y, 1))
    ):
        fin_copy(ss, n, owner_y * 2 + 1 - c, h, sib).wait_recv()
    for owner_y in (y, left_y, right_y, far_y):
        put(owner_y * 2 + 1 - c, 1 - c, owner_y)

    for copy in sends:
        copy.wait_send()

    @pl.loop(0, DIAG)
    def _(j):
        slice_out(j).wait_send()
        far_out(j, right).wait_send()
        near_right(j).wait_send()
        near_left(j).wait_send()
        slice_back(j).wait_send()

    @pl.loop(0, AXIAL)
    def _(j):
        for v in range(RING):
            whole_out(j, v).wait_send()
            whole_back(j, v).wait_send()

    @pl.loop(0, 8)
    def _(i):
        hid_swap(i).wait_send()

    for g in range(3):
        for v in range(RING):
            w_cross(g, v).wait_send()
    for n, peer in enumerate((right, left)):
        part_sum(n, peer).wait_send()
        part_half(n, peer).wait_send()
    for copy in outs:
        copy.wait()


def expert_kernel(tokens, cotangent, ids, probs, w_gate, w_up, w_down):
    tok, features = tokens.shape
    half = features // (2 * RING)
    width = 2 * half
    dma = pltpu.SemaphoreType.DMA
    vmem = pl.BlockSpec(memory_space=pltpu.VMEM)
    hbm = pl.BlockSpec(memory_space=pltpu.HBM)
    return pl.pallas_call(
        kernel,
        out_shape=[jax.ShapeDtypeStruct((tok, features), BF)] * 2,
        in_specs=[hbm] * 2 + [vmem] * 2 + [hbm] * 3,
        out_specs=[hbm] * 2,
        scratch_shapes=[
            pltpu.VMEM((RING, tok, half), BF),
            pltpu.VMEM((RING, tok, half), BF),
            pltpu.VMEM((tok, tok), BF),
            pltpu.VMEM((tok, tok), BF),
            pltpu.VMEM((tok, tok), F32),
            pltpu.VMEM((tok, tok), F32),
            pltpu.VMEM((AXIAL, ROWS, tok), BF),
            pltpu.VMEM((512, tok), F32),
            pltpu.VMEM((3, 256, tok), F32),
            pltpu.VMEM((3, tok, 512), BF),
            pltpu.VMEM((3, 3, tok, 256), BF),
            pltpu.VMEM((DIAG, 9, SLOTS, width), BF),
            pltpu.VMEM((RING, AXIAL, 9, SLOTS, width), BF),
            pltpu.VMEM((RING, 9, PEERS, SLOTS, width), BF),
            pltpu.VMEM((3, RING, 8, 256, half), BF),
            pltpu.VMEM((144, width), BF),
            pltpu.VMEM((128, width), BF),
            pltpu.VMEM((3, 8, 144, 256), F32),
            pltpu.VMEM((3, 8, 144, 128), F32),
            pltpu.VMEM((3, 8, 144, 256), BF),
            pltpu.VMEM((DIAG, 9, SLOTS, width), BF),
            pltpu.VMEM((2, DIAG, 9, SLOTS, width), BF),
            pltpu.VMEM((DIAG, 9, SLOTS, width), BF),
            pltpu.VMEM((RING, AXIAL + 1, 9, SLOTS, width), BF),
            pltpu.VMEM((tok, width), F32),
            pltpu.VMEM((2, tok, width), BF),
            pltpu.VMEM((2, tok, width), BF),
            pltpu.VMEM((2, tok, half), BF),
            pltpu.VMEM((2, tok, half), BF),
            pltpu.VMEM((2 * RING, tok, width), BF),
            dma((2, RING)),
            dma((DIAG,)), dma((DIAG,)),
            dma((RING, AXIAL)), dma((RING, AXIAL)),
            dma((2, DIAG)), dma((2, DIAG)),
            dma((DIAG,)), dma((DIAG,)),
            dma((3, RING)), dma((3, RING)), dma((3, RING)),
            dma((8,)), dma((8,)), dma((8,)), dma((8,)),
            dma((DIAG,)), dma((DIAG,)),
            dma((2, DIAG)), dma((2, DIAG)),
            dma((DIAG,)), dma((DIAG,)),
            dma((RING, AXIAL)), dma((RING, AXIAL)),
            dma((2,)), dma((2,)), dma((2,)), dma((2,)),
            dma((6,)), dma((6,)), dma((8,)), dma((8,)),
            dma((4 * RING,)),
        ],
        compiler_params=pltpu.CompilerParams(
            collective_id=0, has_side_effects=True, vmem_limit_bytes=67_000_000
        ),
    )(tokens, cotangent, ids, probs, w_gate, w_up, w_down)


def body(tokens, cotangent, expert_ids, gate_probs, w_gate, w_up, w_down):
    return tuple(
        expert_kernel(
            tokens, cotangent, expert_ids.T, gate_probs.T, w_gate, w_up, w_down
        )
    )


def solution(mesh):
    return jax.shard_map(
        body,
        mesh=mesh,
        in_specs=(
            P("expert", None),
            P("expert", None),
            P("expert", None),
            P("expert", None),
            P("expert", "tensor", None),
            P("expert", "tensor", None),
            P("expert", "tensor", None),
        ),
        out_specs=(P("expert", None), P("expert", None)),
        check_vma=False,
    )
```

```python
import jax
import jax.numpy as jnp
from jax import lax
from jax.experimental import pallas as pl
from jax.experimental.pallas import tpu as pltpu
from jax.sharding import PartitionSpec as P

BF = jnp.bfloat16
F32 = jnp.float32
RING = 4
PEERS = 16
SLOTS = 8
AXIAL = 6
DIAG = 9
ROWS = 72
MESH = pl.DeviceIdType.MESH


def flat_rows(block):
    return block.astype(F32).reshape(-1, block.shape[-1]).astype(BF)


def kernel(
    tokens, cotangent, ids_ref, probs_ref, wg, wu, wd,
    mixed_ref, grad_ref,
    tok, cot, perm, perm_back, slot_ref, prob_ref, one_d, wrow_d, wrow_g, coll_d, coll_g,
    sendg, sendd, x, wv, xs, xov, acc, accx, hid, rel, own_in, ret, retd, comb, combs, combr, fin,
    tk, g_s, g_r, d_s, d_r, ag_s, ag_r, rl_s, rl_r, wl, wx_s, wx_r,
    ac_s, ac_r, hd_s, hd_r, h_s, h_r, o_s, o_r, b_s, b_r, rd_s, rd_r, cs_s, cs_r,
    f_s, fy_r, fs_r, out_sem,
):
    e, t = lax.axis_index("expert"), lax.axis_index("tensor")
    ez, ex = e // RING, e % RING
    y, c = t // 2, t % 2
    right_y, left_y, far_y = (y + 1) % RING, (y + 3) % RING, (y + 2) % RING
    right, left, sib, far = right_y * 2 + c, left_y * 2 + c, y * 2 + 1 - c, far_y * 2 + c
    half = xs.shape[1] // 2
    core_width = half * RING

    def to_of(k):
        return ((ez + k // RING) % RING) * RING + (ex + k % RING) % RING

    def from_of(k):
        return ((ez + RING - k // RING) % RING) * RING + (ex + RING - k % RING) % RING

    def axial(j):
        return (1 + 2 * (j // 2) - 3 * (j // 4)) * (1 + 3 * (j % 2))

    def diag(j):
        place = (4 * j) % DIAG
        return (1 + place // 3) * RING + 1 + place % 3

    def remote(src, dst, ssem, rsem, pe, pt):
        return pltpu.make_async_remote_copy(
            src_ref=src, dst_ref=dst, send_sem=ssem, recv_sem=rsem,
            device_id={"expert": pe, "tensor": pt}, device_id_type=MESH,
        )

    def signal(pe, pt):
        pl.semaphore_signal(
            pltpu.get_barrier_semaphore(), inc=1,
            device_id={"expert": pe, "tensor": pt}, device_id_type=MESH,
        )

    mats = (wg, wu, wd)
    hu = wg.shape[1]

    def columns(core, v):
        return pl.ds(pl.multiple_of(core * core_width + v * half, half), half)

    def w_local(g, v):
        return pltpu.make_async_copy(
            mats[g].at[:, :, columns(c, v)], wv.at[g, v, :, pl.ds(0, hu), :], wl.at[0]
        )

    def w_cross(g, v):
        return remote(
            mats[g].at[:, :, columns(1 - c, v)], wv.at[g, v, :, pl.ds(128, hu), :],
            wx_s.at[0], wx_r.at[0], e, sib,
        )

    def taken(like, sem):
        pltpu.make_async_copy(like, like, sem).wait()

    def t_local(n, v):
        src, dst = ((tokens, tok), (cotangent, cot))[n]
        return pltpu.make_async_copy(src.at[:, columns(c, v)], dst.at[v], tk.at[n])

    for v in range(RING):
        for n in range(2):
            t_local(n, v).start()

    @pl.loop(1, PEERS)
    def _(k):
        signal(to_of(k), t)

    for other in (right, left, far, sib):
        signal(e, other)

    for g in range(3):
        for v in range(RING):
            w_local(g, v).start()

    count = ids_ref.shape[1]
    lane = lax.broadcasted_iota(jnp.int32, (count, count), 1)
    line = lax.broadcasted_iota(jnp.int32, (count, count), 0)
    chosen = jnp.zeros((count, count), F32)
    prob = jnp.zeros((count, count), F32)
    for k in range(ids_ref.shape[0]):
        match = ids_ref[k:k + 1, :] == line
        chosen = chosen + match.astype(F32)
        prob = prob + jnp.where(match, probs_ref[k:k + 1, :], 0.0)
    before = (line < lane).astype(F32).astype(BF)
    slot = jnp.dot(chosen.astype(BF), before, preferred_element_type=F32)
    slot_ref[...] = jnp.where(chosen > 0.5, slot, -1.0)
    prob_ref[...] = prob
    perm[...] = (lane == (line & 15) * SLOTS + (line >> 4)).astype(F32).astype(BF)
    perm_back[...] = (line == (lane & 15) * SLOTS + (lane >> 4)).astype(F32).astype(BF)

    def row_block(j):
        return pl.ds(pl.multiple_of(j * ROWS, SLOTS), ROWS)

    def build(d):
        block = pl.ds(pl.multiple_of(d * SLOTS, SLOTS), SLOTS)
        slots, weights = slot_ref[block, :], prob_ref[block, :]
        number = lax.broadcasted_iota(jnp.int32, (SLOTS, count), 0).astype(F32)
        place, weight = [], []
        for i in range(SLOTS):
            hit = slots[i:i + 1, :] == number
            place.append(hit.astype(F32))
            weight.append(jnp.where(hit, weights[i:i + 1, :], 0.0))
        hit = slots == float(SLOTS)
        place.append(hit.astype(F32))
        weight.append(jnp.where(hit, weights, 0.0))
        return jnp.concatenate(place, axis=0), jnp.concatenate(weight, axis=0)

    def fill(ref, one, weight, v):
        total = jnp.sum(weight, axis=1, keepdims=True)
        rows = jnp.dot(one, tok[v], preferred_element_type=F32)
        ref[:, :, 0:half] = rows.reshape(9, SLOTS, half).astype(BF)
        rows = jnp.dot(one, cot[v], preferred_element_type=F32) * total
        ref[:, :, half:] = rows.reshape(9, SLOTS, half).astype(BF)

    taken(tok, tk.at[0])
    taken(cot, tk.at[1])

    @pl.loop(0, DIAG)
    def _(j):
        place, weight = build(to_of(diag(j)))
        wrow_g[j // 3, row_block(j % 3), :] = weight
        fill(sendg.at[j], place.astype(BF), weight, y)

    @pl.loop(0, AXIAL)
    def _(j):
        place, weight = build(to_of(axial(j)))
        wrow_d[row_block(j), :] = weight
        one_d[j] = place.astype(BF)

    pl.semaphore_wait(pltpu.get_barrier_semaphore(), PEERS + 3)

    halves = (pl.ds(0, half), pl.ds(half, half))

    def slice_out(j, h):
        src, dst = sendg.at[j, :, :, halves[h]], x.at[y, :, e, :, halves[h]]
        return remote(src, dst, g_s.at[0], g_r.at[h, j], to_of(diag(j)), t)

    def slice_in(j, h):
        src, dst = sendg.at[j, :, :, halves[h]], x.at[y, :, from_of(diag(j)), :, halves[h]]
        return remote(src, dst, g_s.at[0], g_r.at[h, j], to_of(diag(j)), t)

    def whole_out(j, v, h):
        src, dst = sendd.at[v, j, :, :, halves[h]], x.at[v, :, e, :, halves[h]]
        return remote(src, dst, d_s.at[0], d_r.at[h, v], to_of(axial(j)), t)

    for h in range(2):
        @pl.loop(0, DIAG)
        def _(j, h=h):
            slice_out(j, h).start()

    for v in range(RING):
        for g in range(3):
            w_cross(g, v).start()

    def turn(q):
        return (y + RING + 2 * q - 1 - 3 * (q // 3) + (3 - q) // 3) % RING

    def start_whole(h):
        for q in range(RING):
            @pl.loop(0, AXIAL)
            def _(j, q=q):
                whole_out(j, turn(q), h).start()

    def pushed(n, j, h, dst_y, peer):
        s = from_of(diag(j))
        return remote(
            x.at[y, :, s, :, halves[h]], x.at[dst_y, :, s, :, halves[h]],
            ag_s.at[h], ag_r.at[h, j], e, peer,
        )

    def go_right(j, h):
        return pushed(0, j, h, y, right)

    def go_left(j, h):
        return pushed(1, j, h, y, left)

    def relay(j, h, slice_y, peer):
        ref = x.at[slice_y, :, from_of(diag(j)), :, halves[h]]
        return remote(ref, ref, rl_s.at[h], rl_r.at[h], e, peer)

    def relay_any(j, h):
        taken(own_in.at[:, j, :, :, halves[h]], ag_r.at[h, j])

        @pl.when((j + h) % 2 == 0)
        def _():
            relay(j, h, left_y, right).start()

        @pl.when((j + h) % 2 == 1)
        def _():
            relay(j, h, right_y, left).start()

    @pl.loop(0, DIAG)
    def _(j):
        slice_in(j, 0).wait_recv()
        go_right(j, 0).start()
        go_left(j, 0).start()

        @pl.when(j < DIAG - 1)
        def _():
            for u in range(3):
                n = 3 * j + u
                v, jj = turn(n // AXIAL), n % AXIAL
                fill(sendd.at[v, jj], one_d[jj], wrow_d[row_block(jj), :], v)

    start_whole(0)

    @pl.loop(0, DIAG)
    def _(j):
        relay_any(j, 0)

    @pl.loop(0, DIAG)
    def _(j):
        slice_in(j, 1).wait_recv()
        go_right(j, 1).start()
        go_left(j, 1).start()

    start_whole(1)
    place, weight = build(e)
    wrow_d[row_block(AXIAL), :] = weight
    place = place.astype(BF)
    for v in range(RING):
        fill(x.at[v, :, e], place, weight, v)

    zeros = jnp.zeros((8, 16, half), BF)
    for g in range(3):
        for v in range(RING):
            wv[g, v, :, hu:128, :] = zeros
            wv[g, v, :, 128 + hu:256, :] = zeros

    def split(ref, weights):
        weights = weights.T
        hi = weights.astype(BF)
        ref[0] = hi
        ref[1] = (weights - hi.astype(F32)).astype(BF)
        ref[2] = (weights > 0.0).astype(F32).astype(BF)

    wrow_d[(AXIAL + 1) * ROWS:, :] = jnp.zeros((wrow_d.shape[0] - (AXIAL + 1) * ROWS, count), F32)
    split(coll_d, wrow_d[...])
    for n in range(3):
        wrow_g[n, 3 * ROWS:, :] = jnp.zeros((wrow_g.shape[1] - 3 * ROWS, count), F32)
        split(coll_g.at[n], wrow_g[n])

    taken(wv.at[:, :, :, pl.ds(0, hu), :], wl.at[0])
    taken(wv.at[:, :, :, pl.ds(128, hu), :], wx_r.at[0])

    def acc_swap(i, h):
        group = pl.ds(2 * h, 2 - h)
        return remote(
            acc.at[group, i, :, pl.ds(128, 128)], accx.at[group, i], ac_s.at[0], ac_r.at[h, i],
            e, sib,
        )

    def hid_swap(i, h):
        group = pl.ds(h, 1 + h)
        return remote(
            hid.at[group, i, :, pl.ds(0, 128)], hid.at[group, i, :, pl.ds(128, 128)],
            hd_s.at[0], hd_r.at[h, i], e, sib,
        )

    def activate(i, h):
        acc_swap(i, h).wait_recv()
        if h == 0:
            pre = acc[0, i, :, 0:128] + accx[0, i]
            up = acc[1, i, :, 0:128] + accx[1, i]
            sg = jax.nn.sigmoid(pre)
            act = pre * sg
            hid[0, i, :, 0:128] = (act * up).astype(BF)
            acc[0, i, :, 0:128] = up * sg * (1.0 + pre * (1.0 - sg))
            acc[1, i, :, 0:128] = act
        else:
            gh = acc[2, i, :, 0:128] + accx[2, i]
            hid[1, i, :, 0:128] = (gh * acc[0, i, :, 0:128]).astype(BF)
            hid[2, i, :, 0:128] = (gh * acc[1, i, :, 0:128]).astype(BF)
        hid_swap(i, h).start()

    def contract(v, h, start=False, end=False):
        taken(sendd.at[v, :, :, :, halves[h]], d_r.at[h, v])

        over = flat_rows(x[v, 8, :, :, halves[h]])
        xov[:, halves[h]] = jnp.dot(perm[...], over, preferred_element_type=F32).astype(BF)

        @pl.loop(0, 8)
        def _(i):
            xs[0:128, halves[h]] = flat_rows(x[v, i, :, :, halves[h]])
            xs[128:144, halves[h]] = xov[pl.ds(pl.multiple_of(i * 16, 16), 16), halves[h]]
            for g in ((0, 1), (2,))[h]:
                part = lax.dot_general(
                    xs[:, halves[h]], wv[g, v, i], (((1,), (1,)), ((), ())),
                    preferred_element_type=F32,
                )
                if start:
                    acc[g, i] = part
                else:
                    acc[g, i] = acc[g, i] + part
            if end:
                acc_swap(i, h).start()

                @pl.when(i >= 2)
                def _():
                    activate(i - 2, h)

        if end:
            activate(6, h)
            activate(7, h)

    def relay_done(h):
        taken(rel.at[:, :, :, halves[h]], rl_r.at[h])

    def sent(h):
        taken(own_in.at[:, :, :, :, halves[h]], ag_s.at[h])
        taken(rel.at[:, :, :, halves[h]], rl_s.at[h])

    def relay_third(n):
        @pl.loop(3 * n, 3 * n + 3)
        def _(j):
            relay_any(j, 1)

    contract(y, 0, start=True)
    contract(right_y, 0)
    relay_third(0)
    contract(left_y, 0)
    relay_third(1)
    relay_done(0)
    contract(far_y, 0, end=True)
    relay_third(2)
    sent(0)

    def whole_back(j, v, h):
        src = x.at[v, :, from_of(axial(j)), :, halves[h]]
        return remote(
            src, retd.at[v, j, :, :, halves[h]], rd_s.at[0], rd_r.at[h, v],
            from_of(axial(j)), t,
        )

    def expand(v, h, start=False):
        @pl.loop(0, 8)
        def _(i):
            if start:
                hid_swap(i, h).wait_recv()
            if h == 0:
                out = jnp.dot(hid[0, i], wv[2, v, i], preferred_element_type=F32)
            else:
                out = jnp.dot(hid[1, i], wv[0, v, i], preferred_element_type=F32)
                out = out + jnp.dot(hid[2, i], wv[1, v, i], preferred_element_type=F32)
            x[v, i, :, :, halves[h]] = out[0:128].reshape(PEERS, SLOTS, half).astype(BF)
            tail = pl.ds(pl.multiple_of(i * 16, 16), 16)
            xov[tail, halves[h]] = out[128:144].astype(BF)

        over = jnp.dot(perm_back[...], xov[:, halves[h]], preferred_element_type=F32)
        x[v, 8, :, :, halves[h]] = over.reshape(PEERS, SLOTS, half).astype(BF)

    def return_whole(v, h):
        @pl.loop(0, AXIAL)
        def _(j):
            whole_back(j, v, h).start()

    def far_out(j, h, peer):
        src = x.at[far_y, :, from_of(diag(j)), :, halves[h]]
        return remote(src, rel.at[j, :, :, halves[h]], h_s.at[0], h_r.at[h, j], e, peer)

    def near(n, j, h, slice_y, peer):
        return remote(
            x.at[slice_y, :, from_of(diag(j)), :, halves[h]], own_in.at[n, j, :, :, halves[h]],
            o_s.at[0], o_r.at[h, j], e, peer,
        )

    def near_right(j, h):
        return near(0, j, h, right_y, right)

    def near_left(j, h):
        return near(1, j, h, left_y, left)

    def with_relayed(j, h, slice_y):
        far_out(j, h, right).wait_recv()
        s, cols = from_of(diag(j)), halves[h]
        total = x[slice_y, :, s, :, cols].astype(F32) + rel[j, :, :, cols].astype(F32)
        x[slice_y, :, s, :, cols] = total.astype(BF)

    def produce(h):
        expand(far_y, h, start=True)
        for j in range(DIAG):
            far_out(j, h, right if (j + h) % 2 == 0 else left).start()
        return_whole(far_y, h)
        expand(right_y, h)
        for j in range(1 - h, DIAG, 2):
            near_right(j, h).start()
        return_whole(right_y, h)
        expand(left_y, h)
        for j in range(h, DIAG, 2):
            near_left(j, h).start()
        return_whole(left_y, h)
        expand(y, h)
        return_whole(y, h)

    def add_relayed(h):
        @pl.loop(0, DIAG)
        def _(j):
            @pl.when((j + h) % 2 == 0)
            def _():
                with_relayed(j, h, right_y)
                near_right(j, h).start()

            @pl.when((j + h) % 2 == 1)
            def _():
                with_relayed(j, h, left_y)
                near_left(j, h).start()

    def gathered(coll, rows, h):
        width = rows.shape[0]
        if h == 1:
            return jnp.dot(coll[2, :, 0:width], rows, preferred_element_type=F32)
        part = jnp.dot(coll[0, :, 0:width], rows, preferred_element_type=F32)
        return part + jnp.dot(coll[1, :, 0:width], rows, preferred_element_type=F32)

    def whole_sum(v, h):
        retd[v, AXIAL, :, :, halves[h]] = x[v, :, e, :, halves[h]]

        taken(sendd.at[v, :, :, :, halves[h]], rd_r.at[h, v])

        return gathered(coll_d, flat_rows(retd[v, :, :, :, halves[h]]), h)

    def part_sum(n, h, peer):
        return remote(combs.at[h, n], combr.at[h, n], cs_s.at[0], cs_r.at[h], e, peer)

    def part_sums(h):
        for n, (v, peer) in enumerate(((far_y, far), (right_y, right), (left_y, left))):
            combs[h, n] = whole_sum(v, h).astype(BF)
            part_sum(n, h, peer).start()

    def slice_back(j, h):
        s = from_of(diag(j))
        return remote(
            x.at[y, :, s, :, halves[h]], ret.at[j, :, :, halves[h]], b_s.at[0], b_r.at[h, j // 3], s, t
        )

    def own_sums(h, first=0, last=DIAG):
        @pl.loop(first, last)
        def _(j):
            taken(own_in.at[:, j, :, :, halves[h]], o_r.at[h, j])
            s, cols = from_of(diag(j)), halves[h]
            total = x[y, :, s, :, cols].astype(F32) + own_in[0, j, :, :, cols].astype(F32)
            x[y, :, s, :, cols] = (total + own_in[1, j, :, :, cols].astype(F32)).astype(BF)
            slice_back(j, h).start()

    def finish(h):
        total = whole_sum(y, h)
        taken(combr.at[h], cs_r.at[h])
        for n in range(3):
            total = total + combr[h, n].astype(F32)
        comb[...] = total
        for n in range(3):
            taken(ret.at[pl.ds(3 * n, 3), :, :, halves[h]], b_r.at[h, n])
            rows = flat_rows(ret[3 * n:3 * n + 3, :, :, halves[h]])
            comb[...] = comb[...] + gathered(coll_g.at[n], rows, h)
        fin[t, :, halves[h]] = comb[...].astype(BF)

    rows_of = (pl.ds(0, 64), pl.ds(64, 64))
    def fin_y(n, h, slot_t, r, peer):
        ref = fin.at[slot_t, rows_of[r], halves[h]]
        return remote(ref, ref, f_s.at[0], fy_r.at[h, n], e, peer)

    def fin_s(n, h, slot_t, r):
        ref = fin.at[slot_t, rows_of[r], halves[h]]
        return remote(ref, ref, f_s.at[0], fs_r.at[h], e, sib)

    def push(copy):
        copy.start()

    def put(slot_t, owner_c, owner_y, h):
        ref = (mixed_ref, grad_ref)[h]
        pltpu.make_async_copy(
            fin.at[slot_t, :, halves[h]], ref.at[:, columns(owner_c, owner_y)], out_sem.at[h]
        ).start()

    def fin_start(h):
        push(fin_y(0, h, t, 0, right))
        push(fin_y(1, h, t, 1, left))
        push(fin_y(2, h, t, 1, right))
        push(fin_y(3, h, t, 0, left))
        push(fin_s(0, h, t, 0))
        push(fin_s(1, h, t, 1))

    def fin_relay(h):
        fin_y(0, h, left, 0, right).wait_recv()
        push(fin_y(4, h, left, 0, right))
        push(fin_s(2, h, left, 0))
        fin_y(1, h, right, 1, left).wait_recv()
        push(fin_y(5, h, right, 1, left))
        push(fin_s(3, h, right, 1))
        fin_y(2, h, left, 1, right).wait_recv()
        push(fin_s(4, h, left, 1))
        fin_y(3, h, right, 0, left).wait_recv()
        push(fin_s(5, h, right, 0))

    def fin_end(h):
        fin_y(4, h, far, 0, right).wait_recv()
        push(fin_s(6, h, far, 0))
        fin_y(5, h, far, 1, left).wait_recv()
        push(fin_s(7, h, far, 1))

    def fin_put(h):
        for owner_y in (y, left_y, right_y, far_y):
            put(owner_y * 2 + c, c, owner_y, h)
        taken(fin.at[pl.ds(0, RING), :, halves[h]], fs_r.at[h])
        for owner_y in (y, left_y, right_y, far_y):
            put(owner_y * 2 + 1 - c, 1 - c, owner_y, h)

    produce(0)
    contract(y, 1, start=True)
    contract(right_y, 1)
    add_relayed(0)
    contract(left_y, 1)
    relay_done(1)
    contract(far_y, 1, end=True)
    sent(1)
    produce(1)
    own_sums(0)
    part_sums(0)
    add_relayed(1)
    own_sums(1, 0, 6)
    part_sums(1)
    own_sums(1, 6)
    finish(0)
    fin_start(0)
    finish(1)
    fin_start(1)
    fin_relay(0)
    fin_relay(1)
    fin_end(0)
    fin_end(1)
    fin_put(0)
    fin_put(1)

    taken(sendg, g_s.at[0])
    taken(sendd, d_s.at[0])
    taken(wv.at[:, :, :, pl.ds(128, hu), :], wx_s.at[0])
    taken(accx, ac_s.at[0])
    taken(hid.at[:, :, :, pl.ds(0, 128)], hd_s.at[0])
    taken(rel, h_s.at[0])
    taken(own_in, o_s.at[0])
    taken(ret, b_s.at[0])
    taken(sendd, rd_s.at[0])
    taken(combs, cs_s.at[0])
    taken(fin.at[pl.ds(0, 2 * RING - 1)], f_s.at[0])
    taken(mixed_ref, out_sem.at[0])
    taken(grad_ref, out_sem.at[1])


def expert_kernel(tokens, cotangent, ids, probs, w_gate, w_up, w_down):
    tok, features = tokens.shape
    half = features // (2 * RING)
    width = 2 * half
    dma = pltpu.SemaphoreType.DMA
    vmem = pl.BlockSpec(memory_space=pltpu.VMEM)
    hbm = pl.BlockSpec(memory_space=pltpu.HBM)
    return pl.pallas_call(
        kernel,
        out_shape=[jax.ShapeDtypeStruct((tok, features), BF)] * 2,
        in_specs=[hbm] * 2 + [vmem] * 2 + [hbm] * 3,
        out_specs=[hbm] * 2,
        scratch_shapes=[
            pltpu.VMEM((RING, tok, half), BF),
            pltpu.VMEM((RING, tok, half), BF),
            pltpu.VMEM((tok, tok), BF),
            pltpu.VMEM((tok, tok), BF),
            pltpu.VMEM((tok, tok), F32),
            pltpu.VMEM((tok, tok), F32),
            pltpu.VMEM((AXIAL, ROWS, tok), BF),
            pltpu.VMEM((512, tok), F32),
            pltpu.VMEM((3, 256, tok), F32),
            pltpu.VMEM((3, tok, 512), BF),
            pltpu.VMEM((3, 3, tok, 256), BF),
            pltpu.VMEM((DIAG, 9, SLOTS, width), BF),
            pltpu.VMEM((RING, AXIAL, 9, SLOTS, width), BF),
            pltpu.VMEM((RING, 9, PEERS, SLOTS, width), BF),
            pltpu.VMEM((3, RING, 8, 256, half), BF),
            pltpu.VMEM((144, width), BF),
            pltpu.VMEM((128, width), BF),
            pltpu.VMEM((3, 8, 144, 256), F32),
            pltpu.VMEM((3, 8, 144, 128), F32),
            pltpu.VMEM((3, 8, 144, 256), BF),
            pltpu.VMEM((DIAG, 9, SLOTS, width), BF),
            pltpu.VMEM((2, DIAG, 9, SLOTS, width), BF),
            pltpu.VMEM((DIAG, 9, SLOTS, width), BF),
            pltpu.VMEM((RING, AXIAL + 1, 9, SLOTS, width), BF),
            pltpu.VMEM((tok, half), F32),
            pltpu.VMEM((2, 3, tok, half), BF),
            pltpu.VMEM((2, 3, tok, half), BF),
            pltpu.VMEM((2 * RING, tok, width), BF),
            dma((2,)),
            dma((1,)), dma((2, DIAG)),
            dma((1,)), dma((2, RING)),
            dma((2,)), dma((2, DIAG)),
            dma((2,)), dma((2,)),
            dma((1,)), dma((1,)), dma((1,)),
            dma((1,)), dma((2, 8)), dma((1,)), dma((2, 8)),
            dma((1,)), dma((2, DIAG)),
            dma((1,)), dma((2, DIAG)),
            dma((1,)), dma((2, 3)),
            dma((1,)), dma((2, RING)),
            dma((1,)), dma((2,)),
            dma((1,)), dma((2, 6)), dma((2,)),
            dma((2,)),
        ],
        compiler_params=pltpu.CompilerParams(
            collective_id=0, has_side_effects=True, vmem_limit_bytes=67_000_000
        ),
    )(tokens, cotangent, ids, probs, w_gate, w_up, w_down)


def body(tokens, cotangent, expert_ids, gate_probs, w_gate, w_up, w_down):
    return tuple(
        expert_kernel(
            tokens, cotangent, expert_ids.T, gate_probs.T, w_gate, w_up, w_down
        )
    )


def solution(mesh):
    return jax.shard_map(
        body,
        mesh=mesh,
        in_specs=(
            P("expert", None),
            P("expert", None),
            P("expert", None),
            P("expert", None),
            P("expert", "tensor", None),
            P("expert", "tensor", None),
            P("expert", "tensor", None),
        ),
        out_specs=(P("expert", None), P("expert", None)),
        check_vma=False,
    )
```

```python
import jax
import jax.numpy as jnp
from jax import lax
from jax.experimental import pallas as pl
from jax.experimental.pallas import tpu as pltpu
from jax.sharding import PartitionSpec as P

BF = jnp.bfloat16
F32 = jnp.float32
RING = 4
PEERS = 16
SLOTS = 8
AXIAL = 6
DIAG = 9
ROWS = 72
MESH = pl.DeviceIdType.MESH


def flat_rows(block):
    return block.astype(F32).reshape(-1, block.shape[-1]).astype(BF)


def kernel(
    tokens, cotangent, ids_ref, probs_ref, wg, wu, wd,
    mixed_ref, grad_ref,
    tok, cot, perm, perm_back, slot_ref, prob_ref, one_d, wrow_d, wrow_g, coll_d, coll_g,
    sendg, sendd, x, wv, xs, xov, acc, accx, hid, rel, own_in, ret, retd, comb, combs, combr, combf, combh, fin,
    tk, g_s, g_r, d_s, d_r, ag_s, ag_r, rl_s, rl_r, wl, wx_s, wx_r,
    ac_s, ac_r, hd_s, hd_r, h_s, h_r, o_s, o_r, b_s, b_r, rd_s, rd_r, cs_s, cs_r, ch_s, ch_r,
    f_s, fy_r, fs_r, out_sem,
):
    e, t = lax.axis_index("expert"), lax.axis_index("tensor")
    ez, ex = e // RING, e % RING
    y, c = t // 2, t % 2
    right_y, left_y, far_y = (y + 1) % RING, (y + 3) % RING, (y + 2) % RING
    right, left, sib, far = right_y * 2 + c, left_y * 2 + c, y * 2 + 1 - c, far_y * 2 + c
    half = xs.shape[1] // 2
    core_width = half * RING

    def to_of(k):
        return ((ez + k // RING) % RING) * RING + (ex + k % RING) % RING

    def from_of(k):
        return ((ez + RING - k // RING) % RING) * RING + (ex + RING - k % RING) % RING

    def axial(j):
        return (1 + 2 * (j // 2) - 3 * (j // 4)) * (1 + 3 * (j % 2))

    def diag(j):
        place = (7 * j) % DIAG
        return (1 + place // 3) * RING + 1 + place % 3

    def remote(src, dst, ssem, rsem, pe, pt):
        return pltpu.make_async_remote_copy(
            src_ref=src, dst_ref=dst, send_sem=ssem, recv_sem=rsem,
            device_id={"expert": pe, "tensor": pt}, device_id_type=MESH,
        )

    def signal(pe, pt):
        pl.semaphore_signal(
            pltpu.get_barrier_semaphore(), inc=1,
            device_id={"expert": pe, "tensor": pt}, device_id_type=MESH,
        )

    mats = (wg, wu, wd)
    hu = wg.shape[1]

    def columns(core, v):
        return pl.ds(pl.multiple_of(core * core_width + v * half, half), half)

    def w_local(g, v):
        return pltpu.make_async_copy(
            mats[g].at[:, :, columns(c, v)], wv.at[g, v, :, pl.ds(0, hu), :], wl.at[0]
        )

    def w_cross(g, v):
        return remote(
            mats[g].at[:, :, columns(1 - c, v)], wv.at[g, v, :, pl.ds(128, hu), :],
            wx_s.at[0], wx_r.at[0], e, sib,
        )

    def taken(like, sem):
        pltpu.make_async_copy(like, like, sem).wait()

    def t_local(n, v):
        src, dst = ((tokens, tok), (cotangent, cot))[n]
        return pltpu.make_async_copy(src.at[:, columns(c, v)], dst.at[v], tk.at[n])

    for v in range(RING):
        for n in range(2):
            t_local(n, v).start()

    @pl.loop(1, PEERS)
    def _(k):
        signal(to_of(k), t)

    for other in (right, left, sib):
        signal(e, other)

    for g in range(3):
        for v in range(RING):
            w_local(g, v).start()

    count = ids_ref.shape[1]
    lane = lax.broadcasted_iota(jnp.int32, (count, count), 1)
    line = lax.broadcasted_iota(jnp.int32, (count, count), 0)
    chosen = jnp.zeros((count, count), F32)
    prob = jnp.zeros((count, count), F32)
    for k in range(ids_ref.shape[0]):
        match = ids_ref[k:k + 1, :] == line
        chosen = chosen + match.astype(F32)
        prob = prob + jnp.where(match, probs_ref[k:k + 1, :], 0.0)
    before = (line < lane).astype(F32).astype(BF)
    slot = jnp.dot(chosen.astype(BF), before, preferred_element_type=F32)
    slot_ref[...] = jnp.where(chosen > 0.5, slot, -1.0)
    prob_ref[...] = prob
    perm[...] = (lane == (line & 15) * SLOTS + (line >> 4)).astype(F32).astype(BF)
    perm_back[...] = (line == (lane & 15) * SLOTS + (lane >> 4)).astype(F32).astype(BF)

    def row_block(j):
        return pl.ds(pl.multiple_of(j * ROWS, SLOTS), ROWS)

    def build(d):
        block = pl.ds(pl.multiple_of(d * SLOTS, SLOTS), SLOTS)
        slots, weights = slot_ref[block, :], prob_ref[block, :]
        number = lax.broadcasted_iota(jnp.int32, (SLOTS, count), 0).astype(F32)
        place, weight = [], []
        for i in range(SLOTS):
            hit = slots[i:i + 1, :] == number
            place.append(hit.astype(F32))
            weight.append(jnp.where(hit, weights[i:i + 1, :], 0.0))
        hit = slots == float(SLOTS)
        place.append(hit.astype(F32))
        weight.append(jnp.where(hit, weights, 0.0))
        return jnp.concatenate(place, axis=0), jnp.concatenate(weight, axis=0)

    def fill(ref, one, weight, v):
        total = jnp.sum(weight, axis=1, keepdims=True)
        rows = jnp.dot(one, tok[v], preferred_element_type=F32)
        ref[:, :, 0:half] = rows.reshape(9, SLOTS, half).astype(BF)
        rows = jnp.dot(one, cot[v], preferred_element_type=F32) * total
        ref[:, :, half:] = rows.reshape(9, SLOTS, half).astype(BF)

    taken(tok, tk.at[0])
    taken(cot, tk.at[1])

    @pl.loop(0, DIAG)
    def _(j):
        place, weight = build(to_of(diag(j)))
        wrow_g[j // 3, row_block(j % 3), :] = weight
        fill(sendg.at[j], place.astype(BF), weight, y)

    @pl.loop(0, AXIAL)
    def _(j):
        place, weight = build(to_of(axial(j)))
        wrow_d[row_block(j), :] = weight
        one_d[j] = place.astype(BF)

    pl.semaphore_wait(pltpu.get_barrier_semaphore(), PEERS + 2)

    halves = (pl.ds(0, half), pl.ds(half, half))

    def slice_out(j, h):
        src, dst = sendg.at[j, :, :, halves[h]], x.at[y, :, e, :, halves[h]]
        return remote(src, dst, g_s.at[0], g_r.at[h, j], to_of(diag(j)), t)

    def slice_in(j, h):
        src, dst = sendg.at[j, :, :, halves[h]], x.at[y, :, from_of(diag(j)), :, halves[h]]
        return remote(src, dst, g_s.at[0], g_r.at[h, j], to_of(diag(j)), t)

    def whole_out(j, v, h):
        src, dst = sendd.at[v, j, :, :, halves[h]], x.at[v, :, e, :, halves[h]]
        return remote(src, dst, d_s.at[0], d_r.at[h, v], to_of(axial(j)), t)

    for h in range(2):
        @pl.loop(0, DIAG)
        def _(j, h=h):
            slice_out(j, h).start()

    for v in range(RING):
        for g in range(3):
            w_cross(g, v).start()

    def turn(q):
        return (y + RING + 2 * q - 1 - 3 * (q // 3) + (3 - q) // 3) % RING

    def start_whole(h):
        for q in range(RING):
            @pl.loop(0, AXIAL)
            def _(j, q=q):
                whole_out(j, turn(q), h).start()

    def pushed(n, j, h, dst_y, peer):
        s = from_of(diag(j))
        return remote(
            x.at[y, :, s, :, halves[h]], x.at[dst_y, :, s, :, halves[h]],
            ag_s.at[h], ag_r.at[h, j], e, peer,
        )

    def go_right(j, h):
        return pushed(0, j, h, y, right)

    def go_left(j, h):
        return pushed(1, j, h, y, left)

    def relay(j, h, slice_y, peer):
        ref = x.at[slice_y, :, from_of(diag(j)), :, halves[h]]
        return remote(ref, ref, rl_s.at[h], rl_r.at[h], e, peer)

    def relay_any(j, h):
        taken(own_in.at[:, j, :, :, halves[h]], ag_r.at[h, j])

        @pl.when((j + h) % 2 == 0)
        def _():
            relay(j, h, left_y, right).start()

        @pl.when((j + h) % 2 == 1)
        def _():
            relay(j, h, right_y, left).start()

    @pl.loop(0, DIAG)
    def _(j):
        slice_in(j, 0).wait_recv()
        go_right(j, 0).start()
        go_left(j, 0).start()

        @pl.when(j < DIAG - 1)
        def _():
            for u in range(3):
                n = 3 * j + u
                v, jj = turn(n // AXIAL), n % AXIAL
                fill(sendd.at[v, jj], one_d[jj], wrow_d[row_block(jj), :], v)

    start_whole(0)

    @pl.loop(0, DIAG)
    def _(j):
        relay_any(j, 0)

    @pl.loop(0, DIAG)
    def _(j):
        slice_in(j, 1).wait_recv()
        go_right(j, 1).start()
        go_left(j, 1).start()

    start_whole(1)
    place, weight = build(e)
    wrow_d[row_block(AXIAL), :] = weight
    place = place.astype(BF)
    for v in range(RING):
        fill(x.at[v, :, e], place, weight, v)

    zeros = jnp.zeros((8, 16, half), BF)
    for g in range(3):
        for v in range(RING):
            wv[g, v, :, hu:128, :] = zeros
            wv[g, v, :, 128 + hu:256, :] = zeros

    def split(ref, weights):
        weights = weights.T
        hi = weights.astype(BF)
        ref[0] = hi
        ref[1] = (weights - hi.astype(F32)).astype(BF)
        ref[2] = (weights > 0.0).astype(F32).astype(BF)

    wrow_d[(AXIAL + 1) * ROWS:, :] = jnp.zeros((wrow_d.shape[0] - (AXIAL + 1) * ROWS, count), F32)
    split(coll_d, wrow_d[...])
    for n in range(3):
        wrow_g[n, 3 * ROWS:, :] = jnp.zeros((wrow_g.shape[1] - 3 * ROWS, count), F32)
        split(coll_g.at[n], wrow_g[n])

    taken(wv.at[:, :, :, pl.ds(0, hu), :], wl.at[0])
    taken(wv.at[:, :, :, pl.ds(128, hu), :], wx_r.at[0])

    def acc_swap(i, h):
        group = pl.ds(2 * h, 2 - h)
        return remote(
            acc.at[group, i, :, pl.ds(128, 128)], accx.at[group, i], ac_s.at[0], ac_r.at[h, i],
            e, sib,
        )

    def hid_swap(i, h):
        group = pl.ds(h, 1 + h)
        return remote(
            hid.at[group, i, :, pl.ds(0, 128)], hid.at[group, i, :, pl.ds(128, 128)],
            hd_s.at[0], hd_r.at[h, i], e, sib,
        )

    def activate(i, h):
        acc_swap(i, h).wait_recv()
        if h == 0:
            pre = acc[0, i, :, 0:128] + accx[0, i]
            up = acc[1, i, :, 0:128] + accx[1, i]
            sg = jax.nn.sigmoid(pre)
            act = pre * sg
            hid[0, i, :, 0:128] = (act * up).astype(BF)
            acc[0, i, :, 0:128] = up * sg * (1.0 + pre * (1.0 - sg))
            acc[1, i, :, 0:128] = act
        else:
            gh = acc[2, i, :, 0:128] + accx[2, i]
            hid[1, i, :, 0:128] = (gh * acc[0, i, :, 0:128]).astype(BF)
            hid[2, i, :, 0:128] = (gh * acc[1, i, :, 0:128]).astype(BF)
        hid_swap(i, h).start()

    def contract(v, h, start=False, end=False):
        taken(sendd.at[v, :, :, :, halves[h]], d_r.at[h, v])

        over = flat_rows(x[v, 8, :, :, halves[h]])
        xov[:, halves[h]] = jnp.dot(perm[...], over, preferred_element_type=F32).astype(BF)

        @pl.loop(0, 8)
        def _(i):
            xs[0:128, halves[h]] = flat_rows(x[v, i, :, :, halves[h]])
            xs[128:144, halves[h]] = xov[pl.ds(pl.multiple_of(i * 16, 16), 16), halves[h]]
            for g in ((0, 1), (2,))[h]:
                part = lax.dot_general(
                    xs[:, halves[h]], wv[g, v, i], (((1,), (1,)), ((), ())),
                    preferred_element_type=F32,
                )
                if start:
                    acc[g, i] = part
                else:
                    acc[g, i] = acc[g, i] + part
            if end:
                acc_swap(i, h).start()

                @pl.when(i >= 2)
                def _():
                    activate(i - 2, h)

        if end:
            activate(6, h)
            activate(7, h)

    def relay_done(h):
        taken(rel.at[:, :, :, halves[h]], rl_r.at[h])

    def sent(h):
        taken(own_in.at[:, :, :, :, halves[h]], ag_s.at[h])
        taken(rel.at[:, :, :, halves[h]], rl_s.at[h])

    def relay_third(n):
        @pl.loop(3 * n, 3 * n + 3)
        def _(j):
            relay_any(j, 1)

    contract(y, 0, start=True)
    contract(right_y, 0)
    relay_third(0)
    contract(left_y, 0)
    relay_third(1)
    relay_done(0)
    contract(far_y, 0, end=True)
    relay_third(2)
    sent(0)

    def whole_back(j, v, h):
        src = x.at[v, :, from_of(axial(j)), :, halves[h]]
        return remote(
            src, retd.at[v, j, :, :, halves[h]], rd_s.at[0], rd_r.at[h, v],
            from_of(axial(j)), t,
        )

    def expand(v, h, start=False):
        @pl.loop(0, 8)
        def _(i):
            if start:
                hid_swap(i, h).wait_recv()
            if h == 0:
                out = jnp.dot(hid[0, i], wv[2, v, i], preferred_element_type=F32)
            else:
                out = jnp.dot(hid[1, i], wv[0, v, i], preferred_element_type=F32)
                out = out + jnp.dot(hid[2, i], wv[1, v, i], preferred_element_type=F32)
            x[v, i, :, :, halves[h]] = out[0:128].reshape(PEERS, SLOTS, half).astype(BF)
            tail = pl.ds(pl.multiple_of(i * 16, 16), 16)
            xov[tail, halves[h]] = out[128:144].astype(BF)

        over = jnp.dot(perm_back[...], xov[:, halves[h]], preferred_element_type=F32)
        x[v, 8, :, :, halves[h]] = over.reshape(PEERS, SLOTS, half).astype(BF)

    def return_whole(v, h):
        @pl.loop(0, AXIAL)
        def _(j):
            whole_back(j, v, h).start()

    def far_out(j, h, peer):
        src = x.at[far_y, :, from_of(diag(j)), :, halves[h]]
        return remote(src, rel.at[j, :, :, halves[h]], h_s.at[0], h_r.at[h, j], e, peer)

    def near(n, j, h, slice_y, peer):
        return remote(
            x.at[slice_y, :, from_of(diag(j)), :, halves[h]], own_in.at[n, j, :, :, halves[h]],
            o_s.at[0], o_r.at[h, j], e, peer,
        )

    def near_right(j, h):
        return near(0, j, h, right_y, right)

    def near_left(j, h):
        return near(1, j, h, left_y, left)

    def with_relayed(j, h, slice_y):
        far_out(j, h, right).wait_recv()
        s, cols = from_of(diag(j)), halves[h]
        total = x[slice_y, :, s, :, cols].astype(F32) + rel[j, :, :, cols].astype(F32)
        x[slice_y, :, s, :, cols] = total.astype(BF)

    def produce(h):
        expand(far_y, h, start=True)
        for j in range(DIAG):
            far_out(j, h, right if (j + h) % 2 == 0 else left).start()
        return_whole(far_y, h)
        expand(right_y, h)
        for j in range(1 - h, DIAG, 2):
            near_right(j, h).start()
        return_whole(right_y, h)
        expand(left_y, h)
        for j in range(h, DIAG, 2):
            near_left(j, h).start()
        return_whole(left_y, h)
        expand(y, h)
        return_whole(y, h)

    def add_relayed(h):
        @pl.loop(0, DIAG)
        def _(j):
            @pl.when((j + h) % 2 == 0)
            def _():
                with_relayed(j, h, right_y)
                near_right(j, h).start()

            @pl.when((j + h) % 2 == 1)
            def _():
                with_relayed(j, h, left_y)
                near_left(j, h).start()

    def gathered(coll, rows, h):
        width = rows.shape[0]
        if h == 1:
            return jnp.dot(coll[2, :, 0:width], rows, preferred_element_type=F32)
        part = jnp.dot(coll[0, :, 0:width], rows, preferred_element_type=F32)
        return part + jnp.dot(coll[1, :, 0:width], rows, preferred_element_type=F32)

    def whole_sum(v, h):
        retd[v, AXIAL, :, :, halves[h]] = x[v, :, e, :, halves[h]]

        taken(sendd.at[v, :, :, :, halves[h]], rd_r.at[h, v])

        return gathered(coll_d, flat_rows(retd[v, :, :, :, halves[h]]), h)

    def part_sum(n, h, peer):
        return remote(combs.at[h, n], combr.at[h, n], cs_s.at[0], cs_r.at[h], e, peer)

    def part_half(n, h, peer):
        return remote(combf.at[h, n], combh.at[h, n], ch_s.at[0], ch_r.at[h, n], e, peer)

    quarter = half // 2

    def far_sum(h):
        total = whole_sum(far_y, h).astype(BF)
        combf[h, 0] = total[:, 0:quarter]
        combf[h, 1] = total[:, quarter:]
        part_half(0, h, right).start()
        part_half(1, h, left).start()

    def near_sums(h):
        total = whole_sum(right_y, h)
        part_half(0, h, right).wait_recv()
        combs[h, 0, :, 0:quarter] = (total[:, 0:quarter] + combh[h, 0].astype(F32)).astype(BF)
        combs[h, 0, :, quarter:] = total[:, quarter:].astype(BF)
        part_sum(0, h, right).start()
        total = whole_sum(left_y, h)
        part_half(1, h, left).wait_recv()
        combs[h, 1, :, 0:quarter] = total[:, 0:quarter].astype(BF)
        combs[h, 1, :, quarter:] = (total[:, quarter:] + combh[h, 1].astype(F32)).astype(BF)
        part_sum(1, h, left).start()

    def slice_back(j, h):
        s = from_of(diag(j))
        return remote(
            x.at[y, :, s, :, halves[h]], ret.at[j, :, :, halves[h]], b_s.at[0], b_r.at[h, j // 3], s, t
        )

    def own_sums(h, first=0, last=DIAG):
        @pl.loop(first, last)
        def _(j):
            taken(own_in.at[:, j, :, :, halves[h]], o_r.at[h, j])
            s, cols = from_of(diag(j)), halves[h]
            total = x[y, :, s, :, cols].astype(F32) + own_in[0, j, :, :, cols].astype(F32)
            x[y, :, s, :, cols] = (total + own_in[1, j, :, :, cols].astype(F32)).astype(BF)
            slice_back(j, h).start()

    def finish(h):
        total = whole_sum(y, h)
        taken(combr.at[h], cs_r.at[h])
        for n in range(2):
            total = total + combr[h, n].astype(F32)
        comb[...] = total
        for n in range(3):
            taken(ret.at[pl.ds(3 * n, 3), :, :, halves[h]], b_r.at[h, n])
            rows = flat_rows(ret[3 * n:3 * n + 3, :, :, halves[h]])
            comb[...] = comb[...] + gathered(coll_g.at[n], rows, h)
        fin[t, :, halves[h]] = comb[...].astype(BF)

    rows_of = (pl.ds(0, 64), pl.ds(64, 64))
    def fin_y(n, h, slot_t, r, peer):
        ref = fin.at[slot_t, rows_of[r], halves[h]]
        return remote(ref, ref, f_s.at[0], fy_r.at[h, n], e, peer)

    def fin_s(n, h, slot_t, r):
        ref = fin.at[slot_t, rows_of[r], halves[h]]
        return remote(ref, ref, f_s.at[0], fs_r.at[h], e, sib)

    def push(copy):
        copy.start()

    def put(slot_t, owner_c, owner_y, h):
        ref = (mixed_ref, grad_ref)[h]
        pltpu.make_async_copy(
            fin.at[slot_t, :, halves[h]], ref.at[:, columns(owner_c, owner_y)], out_sem.at[h]
        ).start()

    def fin_start(h):
        push(fin_y(0, h, t, 0, right))
        push(fin_y(1, h, t, 1, left))
        push(fin_y(2, h, t, 1, right))
        push(fin_y(3, h, t, 0, left))
        push(fin_s(0, h, t, 0))
        push(fin_s(1, h, t, 1))

    def fin_relay(h):
        fin_y(0, h, left, 0, right).wait_recv()
        push(fin_y(4, h, left, 0, right))
        push(fin_s(2, h, left, 0))
        fin_y(1, h, right, 1, left).wait_recv()
        push(fin_y(5, h, right, 1, left))
        push(fin_s(3, h, right, 1))
        fin_y(2, h, left, 1, right).wait_recv()
        push(fin_s(4, h, left, 1))
        fin_y(3, h, right, 0, left).wait_recv()
        push(fin_s(5, h, right, 0))

    def fin_end(h):
        fin_y(4, h, far, 0, right).wait_recv()
        push(fin_s(6, h, far, 0))
        fin_y(5, h, far, 1, left).wait_recv()
        push(fin_s(7, h, far, 1))

    def fin_put(h):
        for owner_y in (y, left_y, right_y, far_y):
            put(owner_y * 2 + c, c, owner_y, h)
        taken(fin.at[pl.ds(0, RING), :, halves[h]], fs_r.at[h])
        for owner_y in (y, left_y, right_y, far_y):
            put(owner_y * 2 + 1 - c, 1 - c, owner_y, h)

    produce(0)
    contract(y, 1, start=True)
    contract(right_y, 1)
    add_relayed(0)
    contract(left_y, 1)
    relay_done(1)
    contract(far_y, 1, end=True)
    sent(1)
    produce(1)
    own_sums(0)
    far_sum(0)
    add_relayed(1)
    own_sums(1, 0, 6)
    far_sum(1)
    near_sums(0)
    own_sums(1, 6)
    near_sums(1)
    finish(0)
    fin_start(0)
    finish(1)
    fin_start(1)
    fin_relay(0)
    fin_relay(1)
    fin_end(0)
    fin_end(1)
    fin_put(0)
    fin_put(1)

    taken(sendg, g_s.at[0])
    taken(sendd, d_s.at[0])
    taken(wv.at[:, :, :, pl.ds(128, hu), :], wx_s.at[0])
    taken(accx, ac_s.at[0])
    taken(hid.at[:, :, :, pl.ds(0, 128)], hd_s.at[0])
    taken(rel, h_s.at[0])
    taken(own_in, o_s.at[0])
    taken(ret, b_s.at[0])
    taken(sendd, rd_s.at[0])
    taken(combs, cs_s.at[0])
    taken(combf, ch_s.at[0])
    taken(fin.at[pl.ds(0, 2 * RING - 1)], f_s.at[0])
    taken(mixed_ref, out_sem.at[0])
    taken(grad_ref, out_sem.at[1])


def expert_kernel(tokens, cotangent, ids, probs, w_gate, w_up, w_down):
    tok, features = tokens.shape
    half = features // (2 * RING)
    width = 2 * half
    dma = pltpu.SemaphoreType.DMA
    vmem = pl.BlockSpec(memory_space=pltpu.VMEM)
    hbm = pl.BlockSpec(memory_space=pltpu.HBM)
    return pl.pallas_call(
        kernel,
        out_shape=[jax.ShapeDtypeStruct((tok, features), BF)] * 2,
        in_specs=[hbm] * 2 + [vmem] * 2 + [hbm] * 3,
        out_specs=[hbm] * 2,
        scratch_shapes=[
            pltpu.VMEM((RING, tok, half), BF),
            pltpu.VMEM((RING, tok, half), BF),
            pltpu.VMEM((tok, tok), BF),
            pltpu.VMEM((tok, tok), BF),
            pltpu.VMEM((tok, tok), F32),
            pltpu.VMEM((tok, tok), F32),
            pltpu.VMEM((AXIAL, ROWS, tok), BF),
            pltpu.VMEM((512, tok), F32),
            pltpu.VMEM((3, 256, tok), F32),
            pltpu.VMEM((3, tok, 512), BF),
            pltpu.VMEM((3, 3, tok, 256), BF),
            pltpu.VMEM((DIAG, 9, SLOTS, width), BF),
            pltpu.VMEM((RING, AXIAL, 9, SLOTS, width), BF),
            pltpu.VMEM((RING, 9, PEERS, SLOTS, width), BF),
            pltpu.VMEM((3, RING, 8, 256, half), BF),
            pltpu.VMEM((144, width), BF),
            pltpu.VMEM((128, width), BF),
            pltpu.VMEM((3, 8, 144, 256), F32),
            pltpu.VMEM((3, 8, 144, 128), F32),
            pltpu.VMEM((3, 8, 144, 256), BF),
            pltpu.VMEM((DIAG, 9, SLOTS, width), BF),
            pltpu.VMEM((2, DIAG, 9, SLOTS, width), BF),
            pltpu.VMEM((DIAG, 9, SLOTS, width), BF),
            pltpu.VMEM((RING, AXIAL + 1, 9, SLOTS, width), BF),
            pltpu.VMEM((tok, half), F32),
            pltpu.VMEM((2, 2, tok, half), BF),
            pltpu.VMEM((2, 2, tok, half), BF),
            pltpu.VMEM((2, 2, tok, half // 2), BF),
            pltpu.VMEM((2, 2, tok, half // 2), BF),
            pltpu.VMEM((2 * RING, tok, width), BF),
            dma((2,)),
            dma((1,)), dma((2, DIAG)),
            dma((1,)), dma((2, RING)),
            dma((2,)), dma((2, DIAG)),
            dma((2,)), dma((2,)),
            dma((1,)), dma((1,)), dma((1,)),
            dma((1,)), dma((2, 8)), dma((1,)), dma((2, 8)),
            dma((1,)), dma((2, DIAG)),
            dma((1,)), dma((2, DIAG)),
            dma((1,)), dma((2, 3)),
            dma((1,)), dma((2, RING)),
            dma((1,)), dma((2,)),
            dma((1,)), dma((2, 2)),
            dma((1,)), dma((2, 6)), dma((2,)),
            dma((2,)),
        ],
        compiler_params=pltpu.CompilerParams(
            collective_id=0, has_side_effects=True, vmem_limit_bytes=67_000_000
        ),
    )(tokens, cotangent, ids, probs, w_gate, w_up, w_down)


def copy_kernel(mixed_in, grad_in, mixed_ref, grad_ref, buf, in_sem, out_sem):
    parts = buf.shape[1]
    rows = buf.shape[2]
    pairs = [
        (n, p, src.at[pl.ds(p * rows, rows), :], dst.at[pl.ds(p * rows, rows), :])
        for p in range(parts)
        for n, (src, dst) in enumerate(((mixed_in, mixed_ref), (grad_in, grad_ref)))
    ]
    for n, p, src, _ in pairs:
        pltpu.make_async_copy(src, buf.at[n, p], in_sem.at[n, p]).start()
    for n, p, src, dst in pairs:
        pltpu.make_async_copy(src, buf.at[n, p], in_sem.at[n, p]).wait()
        pltpu.make_async_copy(buf.at[n, p], dst, out_sem.at[n, p]).start()
    for n, p, _, dst in pairs:
        pltpu.make_async_copy(buf.at[n, p], dst, out_sem.at[n, p]).wait()


def copy_out(mixed, grad):
    parts = 4
    hbm = pl.BlockSpec(memory_space=pltpu.HBM)
    rows, width = mixed.shape
    return pl.pallas_call(
        copy_kernel,
        out_shape=[jax.ShapeDtypeStruct(mixed.shape, mixed.dtype)] * 2,
        in_specs=[hbm] * 2,
        out_specs=[hbm] * 2,
        scratch_shapes=[
            pltpu.VMEM((2, parts, rows // parts, width), mixed.dtype),
            pltpu.SemaphoreType.DMA((2, parts)),
            pltpu.SemaphoreType.DMA((2, parts)),
        ],
    )(mixed, grad)


def body(tokens, cotangent, expert_ids, gate_probs, w_gate, w_up, w_down):
    mixed, grad = expert_kernel(
        tokens, cotangent, expert_ids.T, gate_probs.T, w_gate, w_up, w_down
    )
    return tuple(copy_out(mixed, grad))


def solution(mesh):
    return jax.shard_map(
        body,
        mesh=mesh,
        in_specs=(
            P("expert", None),
            P("expert", None),
            P("expert", None),
            P("expert", None),
            P("expert", "tensor", None),
            P("expert", "tensor", None),
            P("expert", "tensor", None),
        ),
        out_specs=(P("expert", None), P("expert", None)),
        check_vma=False,
    )
```
